256 devices in a mesh: expert: 64 (over y, z, core), etp: 4 (over x).
Axes of the slice: x: 4, y: 4, z: 8, core: 2. Of those that a mesh axis runs over, the one named last changes fastest.
Arguments:
- tokens: bfloat16 [8192, 2048], P('expert'), may hold values from -6 to 6
- grad_out: bfloat16 [8192, 2048], P('expert'), may hold values from -6 to 6
- routes: int32 [8192, 8], P('expert'), may hold values from 0 to 127, all different within a row; in each aligned block of 128 rows (0 to 127, 128 to 255, ...) at most 10 rows name the same one
- probs: bfloat16 [8192, 8], P('expert'), may hold values from 0.049804688 to 0.3984375
- w_gate: bfloat16 [128, 768, 2048], P('expert', 'etp'), may hold values from -0.125 to 0.125
- w_up: bfloat16 [128, 768, 2048], P('expert', 'etp'), may hold values from -0.125 to 0.125
- w_down: bfloat16 [128, 768, 2048], P('expert', 'etp'), may hold values from -0.21875 to 0.21875
Outputs:
- grad_tokens: bfloat16 [8192, 2048], P('expert')
- grad_probs: bfloat16 [8192, 8], P('expert')
- grad_gate: bfloat16 [128, 768, 2048], P('expert', 'etp')
- grad_up: bfloat16 [128, 768, 2048], P('expert', 'etp')
- grad_down: bfloat16 [128, 768, 2048], P('expert', 'etp')
The draws below stay inside these ranges and needn't reach their ends.
Inputs may be any that keep to these rules, and one draw needn't show every extreme that they name: `routes`: each row names 8 different experts. Among the 128 rows of one device no expert is named by more than 10 rows, a bound that some block reaches.
All inputs are finite; a program needn't handle non-finite values.
Results may differ from the reference program's by a relative error of at most 0.018.
Values may be sent and summed in bfloat16 or wider, within the bound.
A program may use at most 128 MiB of HBM per device.

```python
import math
import jax
import jax.numpy as jnp
import numpy as np
from jax import lax

D = 2048
FF = 768
TOP = 8
TOK_DEV = 128
EXPERTS = 128
TOKENS = 8192
MOST = 10
HID_DEV = 192
N_EXPERT = 64
N_ETP = 4


def steps_of(stream_key, dims, cuts, low, high):
    loudness, own = 1.0, jax.random.fold_in(stream_key, 6)
    for dim, shards_of in cuts:
        heights = jnp.exp(jax.random.uniform(jax.random.fold_in(own, dim), (shards_of,), jnp.float32, low / len(cuts), high / len(cuts)))
        loudness = loudness * jnp.repeat(heights, dims[dim] // shards_of).reshape([-1 if axis == dim else 1 for axis in range(len(dims))])
    return loudness


def routed_block(own_key, own, number, rows, count, top, reach, lean):
    sequence = jax.random.permutation(own_key, count)
    packed, ordinary = shares(count, rows * top, reach, lean, True), shares(count, rows * top, reach, lean, False)
    places = jnp.arange(count)

    def named(sizes, offset_by):
        used = int((sizes > 0).sum())
        fixed = max(1, used // 4)
        passed = fixed + (places - fixed + offset_by * (used - fixed)) % max(1, count - fixed)
        return jnp.zeros((count,), jnp.int32).at[sequence[jnp.where(places < fixed, places, passed)]].set(jnp.asarray(sizes, jnp.int32))

    sizes = jnp.where(number % 4 == 0, named(packed, number // 4), named(ordinary, number - number // 4 - 1))
    mixed = jax.random.permutation(jax.random.fold_in(own, 3), count)
    source_of, taker = mixed[0:count // 2 * 2:2], mixed[1:count // 2 * 2:2]
    room = jnp.minimum(sizes[source_of] - 1, reach - sizes[taker]) // 2
    room = jnp.where((source_of == sequence[0]) | (taker == sequence[0]) | (sizes[taker] == 0), 0, jnp.maximum(room, 0))
    passed = jax.random.randint(jax.random.fold_in(own, 4), (count // 2,), 0, 1 << 20) % (room + 1)
    sizes = sizes.at[source_of].add(-passed).at[taker].add(passed)
    members = jnp.searchsorted(jnp.cumsum(sizes), jnp.arange(rows * top), side="right").astype(jnp.int32)
    grid = members.reshape(top, rows).T
    grid = grid[jax.random.permutation(jax.random.fold_in(own, 1), rows)]
    offset_by = jax.random.randint(jax.random.fold_in(own, 2), (rows, 1), 0, top)
    return jnp.take_along_axis(grid, (jnp.arange(top)[None, :] + offset_by) % top, axis=1)


def shares(number_of, total, bound, slope, full):
    portions = [(1 << 20) // math.isqrt(grade ** slope) + 1 for grade in range(1, number_of + 1)]
    largest = bound if full else min(bound, max(-(-total // number_of), total * portions[0] // sum(portions)))
    least = 1 if total - largest >= number_of - 1 else 0
    given, rest = [largest] + [least] * (number_of - 1), total - largest - least * (number_of - 1)
    while rest > 0:
        movable = [i for i in range(1, number_of) if given[i] < largest] or [i for i in range(1, number_of) if given[i] < bound]
        pool, budget = sum([portions[i] for i in movable]), rest
        for i in movable:
            extra = min(bound - given[i], max(1, budget * portions[i] // pool), rest)
            given[i] = given[i] + extra
            rest = rest - extra
    return np.array(given)


def scatter_about(key, shape, width, most, split=(), kind=jnp.bfloat16):
    gain = steps_of(key, shape, split, -0.22, 0.18) if split else 1.0
    result = jax.random.normal(key, shape, jnp.float32) * width * gain
    return jnp.minimum(jnp.maximum(result, -most), most).astype(kind)


def setup_inputs(seed: int = 0) -> dict:
    seeds = jax.random.split(jax.random.key(seed), 8)
    tokens = scatter_about(seeds[0], (TOKENS, D), 1.0, 6.0, ((0, 64),))
    grad_out = scatter_about(seeds[1], (TOKENS, D), 1.0, 6.0, ((0, 64),))
    routes_keys = jax.random.split(jax.random.fold_in(seeds[2], 1), TOKENS // TOK_DEV)
    routes_turns = jax.random.permutation(jax.random.fold_in(seeds[2], 3), TOKENS // TOK_DEV)
    routes = jax.vmap(lambda own, number: routed_block(jax.random.fold_in(seeds[2], 2), own, number, TOK_DEV, EXPERTS, TOP, MOST, 2))(routes_keys, routes_turns).reshape((TOKENS, TOP))
    probs = jnp.clip(0.049804688 + 0.3486328 * jax.random.uniform(seeds[3], (TOKENS, TOP), jnp.float32) ** steps_of(seeds[3], (TOKENS, TOP), ((0, 64),), -0.2, 0.2), 0.049804688, 0.3984375).astype(jnp.bfloat16)
    w_gate = scatter_about(seeds[4], (EXPERTS, FF, D), D ** -0.5, 0.125, ((0, 64), (1, 4)))
    w_up = scatter_about(seeds[5], (EXPERTS, FF, D), D ** -0.5, 0.125, ((0, 64), (1, 4)))
    w_down = scatter_about(seeds[6], (EXPERTS, FF, D), FF ** -0.5, 0.21875, ((0, 64), (1, 4)))
    return dict(tokens=tokens, grad_out=grad_out, routes=routes, probs=probs, w_gate=w_gate, w_up=w_up, w_down=w_down)


def reference(tokens, grad_out, routes, probs, w_gate, w_up, w_down):
    expert_count = w_gate.shape[0]
    capacity = N_EXPERT * MOST
    pair_count = TOKENS * TOP
    shard_count = N_ETP
    flat_routes = routes.reshape(-1).astype(jnp.int32)
    sort_order = jnp.argsort(flat_routes, stable=True).astype(jnp.int32)
    ordered = flat_routes[sort_order]
    counts = jnp.zeros((expert_count,), jnp.int32).at[flat_routes].add(1)
    starts = jnp.cumsum(counts) - counts
    position = jnp.arange(pair_count, dtype=jnp.int32) - starts[ordered]
    slot_table = jnp.full((expert_count, capacity), pair_count, jnp.int32).at[ordered, position].set(sort_order)
    prob_flat = probs.reshape(-1)

    def expert_step(carried, inputs):
        grad_acc, prob_acc = carried
        index_row, gate_w, up_w, down_w = inputs
        filled = index_row < pair_count
        safe_index = jnp.where(filled, index_row, 0)
        token_of = safe_index // TOP
        row_vals = jnp.where(filled[:, None], tokens[token_of], 0)
        grad_vals = jnp.where(filled[:, None], grad_out[token_of], 0)
        weight = jnp.where(filled, prob_flat[safe_index], 0).astype(jnp.float32)[:, None]
        pre_gate = jnp.dot(row_vals, gate_w.T, preferred_element_type=jnp.float32)
        pre_up = jnp.dot(row_vals, up_w.T, preferred_element_type=jnp.float32)
        back_grad = jnp.dot(grad_vals, down_w.T, preferred_element_type=jnp.float32)
        sigma_gate = jax.nn.sigmoid(pre_gate)
        activated = pre_gate * sigma_gate
        hidden = (activated * pre_up).astype(jnp.bfloat16)
        prob_part = jnp.sum((hidden.astype(jnp.float32) * back_grad).reshape(capacity, shard_count, HID_DEV), axis=-1).astype(jnp.bfloat16)
        prob_vals = jnp.sum(prob_part.astype(jnp.float32), axis=1).astype(jnp.bfloat16)
        scaled = (weight * grad_vals.astype(jnp.float32)).astype(jnp.bfloat16)
        down_grad = jnp.dot(hidden.T, scaled, preferred_element_type=jnp.float32).astype(jnp.bfloat16)
        hidden_grad = weight * back_grad
        d_gate = (hidden_grad * pre_up * sigma_gate * (1.0 + pre_gate * (1.0 - sigma_gate))).astype(jnp.bfloat16)
        d_up = (hidden_grad * activated).astype(jnp.bfloat16)
        gate_grad = jnp.dot(d_gate.T, row_vals, preferred_element_type=jnp.float32).astype(jnp.bfloat16)
        up_grad = jnp.dot(d_up.T, row_vals, preferred_element_type=jnp.float32).astype(jnp.bfloat16)
        gate_parts = jnp.einsum("cgh,ghd->cgd", d_gate.astype(jnp.float32).reshape(capacity, shard_count, HID_DEV), gate_w.astype(jnp.float32).reshape(shard_count, HID_DEV, D))
        up_parts = jnp.einsum("cgh,ghd->cgd", d_up.astype(jnp.float32).reshape(capacity, shard_count, HID_DEV), up_w.astype(jnp.float32).reshape(shard_count, HID_DEV, D))
        row_part = (gate_parts + up_parts).astype(jnp.bfloat16)
        pair_grad = jnp.sum(row_part.astype(jnp.float32), axis=1).astype(jnp.bfloat16)
        token_target = jnp.where(filled, token_of, TOKENS)
        grad_acc = grad_acc.at[token_target].add(pair_grad.astype(jnp.float32), mode="drop")
        prob_acc = prob_acc.at[index_row].set(prob_vals, mode="drop")
        return (grad_acc, prob_acc), (gate_grad, up_grad, down_grad)

    initial = (jnp.zeros((TOKENS, D), jnp.float32), jnp.zeros((pair_count,), jnp.bfloat16))
    (grad_acc, prob_acc), (grad_gate, grad_up, grad_down) = lax.scan(expert_step, initial, (slot_table, w_gate, w_up, w_down))
    return grad_acc.astype(jnp.bfloat16), prob_acc.reshape(TOKENS, TOP), grad_gate, grad_up, grad_down
```

```python
import jax
import jax.numpy as jnp
from jax import lax
from jax.sharding import Mesh, PartitionSpec as P

NY, NZ, NC, NX = 4, 8, 2, 4
SLOTS = 10
BF = jnp.bfloat16
F32 = jnp.float32


def dot(spec, a, b):
    return jnp.einsum(spec, a, b, preferred_element_type=F32)


def body(tokens, grad_out, routes, probs, w_gate, w_up, w_down):
    tok_rows, top_count = routes.shape
    width = tokens.shape[1]
    half = width // 2
    quarter = width // 4
    le = w_gate.shape[0]
    hid = w_gate.shape[1]
    sources = NZ * NC
    z = lax.axis_index("z")
    c = lax.axis_index("c")
    x = lax.axis_index("x")
    h = x % 2
    mine = jnp.concatenate(
        [
            lax.dynamic_slice_in_dim(tokens, h * half, half, axis=1),
            lax.dynamic_slice_in_dim(grad_out, h * half, half, axis=1),
        ],
        axis=1,
    )
    around = lax.all_gather(mine, ("z", "c"), axis=0, tiled=False)
    info = jnp.concatenate([routes.astype(BF), probs], axis=1)
    info_all = lax.all_gather(info, ("z", "c"), axis=0, tiled=False)
    routes_all = info_all[:, :, :top_count].astype(jnp.int32)
    probs_all = info_all[:, :, top_count:]
    ys = jnp.arange(NY)[:, None]
    experts = (((ys * NZ + z) * NC + c) * le + jnp.arange(le)[None, :]).reshape(-1)
    hit = routes_all[None] == experts[:, None, None, None]
    named = jnp.any(hit, axis=-1)
    weight = jnp.sum(jnp.where(hit, probs_all[None].astype(F32), 0), axis=-1)
    before = (jnp.arange(tok_rows)[:, None] < jnp.arange(tok_rows)[None, :]).astype(BF)
    rank = dot("est,tu->esu", named.astype(BF), before)
    pick = named[:, :, None, :] & (
        rank[:, :, None, :] == jnp.arange(SLOTS, dtype=F32)[None, None, :, None]
    )
    pick_w = jnp.where(pick, weight[:, :, None, :], 0).astype(BF)
    pick = pick.astype(BF)
    rows_x = dot("esjt,std->esjd", pick, around[..., :half]).astype(BF)
    rows_o = dot("esjt,std->esjd", pick_w, around[..., half:]).astype(BF)
    rows = jnp.concatenate([rows_x, rows_o], axis=-1).reshape(
        NY, le, sources * SLOTS, width
    )
    rows = lax.all_to_all(rows, "y", split_axis=0, concat_axis=0, tiled=True)
    rows = jnp.transpose(rows, (1, 0, 2, 3)).reshape(le, NY * sources * SLOTS, 4, quarter)
    up_ring = [(i, (i + 1) % NX) for i in range(NX)]
    down_ring = [(i, (i + NX - 1) % NX) for i in range(NX)]
    first = lax.ppermute(rows[:, :, 0::2], "x", up_ring)
    second = lax.ppermute(rows[:, :, 1::2], "x", down_ring)

    def joined(i):
        mine_h = rows[:, :, 2 * i : 2 * i + 2].reshape(rows.shape[:2] + (half,))
        other = jnp.concatenate([first[:, :, i], second[:, :, i]], axis=-1)
        return jnp.where(
            h == 0,
            jnp.concatenate([mine_h, other], -1),
            jnp.concatenate([other, mine_h], -1),
        )

    in_rows, scaled = joined(0), joined(1)
    pre_gate = dot("end,ehd->enh", in_rows, w_gate)
    pre_up = dot("end,ehd->enh", in_rows, w_up)
    back = dot("end,ehd->enh", scaled, w_down)
    sig = jax.nn.sigmoid(pre_gate)
    act = pre_gate * sig
    hidden = (act * pre_up).astype(BF)
    prob_local = jnp.sum(hidden.astype(F32) * back, axis=-1)
    grad_down = dot("enh,end->ehd", hidden, scaled).astype(BF)
    d_gate = (back * pre_up * sig * (1.0 + pre_gate * (1.0 - sig))).astype(BF)
    d_up = (back * act).astype(BF)
    grad_gate = dot("enh,end->ehd", d_gate, in_rows).astype(BF)
    grad_up = dot("enh,end->ehd", d_up, in_rows).astype(BF)
    part = (dot("enh,ehd->end", d_gate, w_gate) + dot("enh,ehd->end", d_up, w_up)).astype(BF)
    part = part.reshape(le, NY * sources * SLOTS, 2, 2, quarter)
    keep = jnp.where(h == 0, part[:, :, 0], part[:, :, 1])
    give = jnp.where(h == 0, part[:, :, 1], part[:, :, 0])
    got_first = lax.ppermute(give[:, :, 0], "x", up_ring)
    got_second = lax.ppermute(give[:, :, 1], "x", down_ring)
    kept = jnp.concatenate(
        [
            keep[:, :, 0].astype(F32) + got_first.astype(F32),
            keep[:, :, 1].astype(F32) + got_second.astype(F32),
        ],
        axis=-1,
    ).astype(BF)
    kept = jnp.transpose(kept.reshape(le, NY, sources * SLOTS, half), (1, 0, 2, 3))
    kept = lax.all_to_all(kept, "y", split_axis=0, concat_axis=0, tiled=True)
    kept = kept.reshape(NY * le, sources, SLOTS, half)
    prob_rows = jnp.transpose(prob_local.reshape(le, NY, sources * SLOTS), (1, 0, 2)).astype(BF)
    prob_rows = lax.all_to_all(prob_rows, "y", split_axis=0, concat_axis=0, tiled=True)
    prob_rows = prob_rows.reshape(NY * le, sources, SLOTS)
    home = dot("esjt,esjd->std", pick, kept).astype(BF)
    home = lax.psum_scatter(home, ("z", "c"), scatter_dimension=0, tiled=False)
    prob_tok = dot("esjt,esj->set", pick, prob_rows).astype(BF)
    prob_tok = lax.all_to_all(prob_tok, ("z", "c"), split_axis=0, concat_axis=0, tiled=True)
    prob_tok = lax.psum(prob_tok.astype(F32), "x")
    zeros = jnp.zeros_like(home)
    wide = jnp.where(
        h == 0, jnp.concatenate([home, zeros], -1), jnp.concatenate([zeros, home], -1)
    )
    grad_tokens = lax.psum(wide, "x")
    by_expert = jnp.transpose(
        prob_tok.reshape(NZ * NC, NY, le, tok_rows), (1, 0, 2, 3)
    ).reshape(-1, tok_rows)
    chosen = routes[:, :, None] == jnp.arange(by_expert.shape[0])[None, None, :]
    total = jnp.sum(jnp.where(chosen, by_expert.T[:, None, :], 0), axis=-1)
    grad_probs = (total / probs.astype(F32)).astype(BF)
    return (grad_tokens, grad_probs, grad_gate, grad_up, grad_down)


def solution(mesh):
    cut = Mesh(mesh.devices.reshape(NY, NZ, NC, NX), ("y", "z", "c", "x"))
    rows = P(("y", "z", "c"), None)
    weights = P(("y", "z", "c"), "x", None)
    return jax.shard_map(
        body,
        mesh=cut,
        in_specs=(rows, rows, rows, rows, weights, weights, weights),
        out_specs=(rows, rows, weights, weights, weights),
        check_vma=False,
    )
```

```python
import functools

import jax
import jax.numpy as jnp
from jax import lax
from jax.experimental import pallas as pl
from jax.experimental.pallas import tpu as pltpu
from jax.sharding import Mesh, PartitionSpec as P

NY, NZ, NC, NX = 4, 8, 2, 4
SLOTS = 10
LE = 2
TOK = 128
GROUP = 4 * NC * SLOTS
LANES = 512
BF = jnp.bfloat16
F32 = jnp.float32
MESH = pl.DeviceIdType.MESH
PLACE = {0: 0, 1: 1, 7: 2, 2: 3, 6: 4, 3: 5, 5: 6, 4: 7}


def remote(src, dst, send, recv, **where):
    return pltpu.make_async_remote_copy(
        src_ref=src, dst_ref=dst, send_sem=send, recv_sem=recv, device_id=where, device_id_type=MESH
    )


def axes():
    return tuple(lax.axis_index(n) for n in ("y", "z", "c", "x"))


def dispatch_kernel(
    mine, info, rows, pick_out,
    blocks, infos, pick_w, out_y, relay,
    i_send, i_recv, z_send, z_recv, p_send, p_recv, y_send, y_recv, r_send, r_recv, x_send, x_recv, l_sem, s_sem,
):
    y, z, c, x = axes()
    h = x % 2
    other = 1 - c
    sign = 1 - 2 * c
    z_long, z_short = (z + sign + NZ) % NZ, (z - sign + NZ) % NZ
    y_up, y_down = (y + 1) % NY, (y + NY - 1) % NY
    x_up, x_down = (x + 1) % NX, (x + NX - 1) % NX

    barrier = pltpu.get_barrier_semaphore()
    for m in range(NZ):
        for cc in ((c, other) if m else (other,)):
            pl.semaphore_signal(barrier, inc=1, device_id={"z": (z + m) % NZ, "c": cc}, device_id_type=MESH)
    for yy in (y_up, y_down):
        pl.semaphore_signal(barrier, inc=1, device_id={"y": yy}, device_id_type=MESH)
    for xx in (x_up, x_down):
        pl.semaphore_signal(barrier, inc=1, device_id={"x": xx}, device_id_type=MESH)
    pl.semaphore_wait(barrier, 2 * NZ - 1 + 4)

    waits = []

    def go(copy):
        copy.start()
        waits.append(copy)

    def info_copy(m, cc, far):
        at = PLACE[(NZ - m) % NZ]
        return remote(
            info, infos.at[at, c], i_send.at[m, far], i_recv.at[at, c], z=(z + m) % NZ, c=cc
        )

    for m in range(NZ):
        if m:
            go(info_copy(m, c, 0))
        go(info_copy(m, other, 1))

    def place(long, s):
        if s == 0:
            return 0
        if long:
            return 7 if s == 4 else 2 * s - c
        return 2 * s - 1 + c

    def hop(k, long, s):
        index = (s - 1) if long else (3 + s)
        src = mine.at[k] if s == 1 else blocks.at[k, place(long, s - 1), c]
        return remote(
            src, blocks.at[k, place(long, s), c], z_send.at[k, index], z_recv.at[k, index],
            z=z_long if long else z_short,
        )

    def to_partner(k, at):
        src = mine.at[k] if isinstance(at, int) and at == 0 else blocks.at[k, at, c]
        return remote(src, blocks.at[k, at, c], p_send.at[k, at], p_recv.at[k, at], c=other)

    def start_chunk(k):
        go(hop(k, True, 1))
        go(hop(k, False, 1))
        go(to_partner(k, 0))
        keep = pltpu.make_async_copy(mine.at[k], blocks.at[k, 0, c], l_sem.at[k])
        keep.start()
        return keep

    keeps = {0: start_chunk(0)}

    def z_step(k, s):
        for long in ((True, False) if s < 4 else (True,)):
            hop(k, long, s).wait_recv()
            if s < (4 if long else 3):
                go(hop(k, long, s + 1))
            go(to_partner(k, place(long, s)))

    def y_piece(k, g, d, le):
        src = out_y.at[k, g, d, le]
        slot = 4 * (k // 2) + 2 * h + k % 2
        landing = rows.at[slot, le, y, g]
        sems = dict(send=y_send.at[k, g, d - 1, le], recv=y_recv.at[k, g, d - 1, le])
        if d == 1:
            return remote(src, landing, y=y_up, **sems)
        if d == 3:
            return remote(src, landing, y=y_down, **sems)
        return remote(src, relay.at[k, g, le], y=y_up if le == 0 else y_down, **sems)

    def relayed(k, g, le):
        slot = 4 * (k // 2) + 2 * h + k % 2
        came = y_down if le == 0 else y_up
        return remote(
            relay.at[k, g, le], rows.at[slot, le, came, g], r_send.at[k, g, le], r_recv.at[k, g, le],
            y=y_up if le == 0 else y_down,
        )

    def x_piece(k, g, d, le):
        slot = 4 * (k // 2) + 2 * h + k % 2
        there = rows.at[slot, le, (y + NY - d) % NY, g]
        src = out_y.at[k, g, 0, le] if d == 0 else there
        return remote(
            src, there, x_send.at[k, g, d, le], x_recv.at[k, g, d, le], x=x_up if le == 0 else x_down
        )

    def own_piece(k, g, le):
        slot = 4 * (k // 2) + 2 * h + k % 2
        return pltpu.make_async_copy(
            out_y.at[k, g, 0, le], rows.at[slot, le, y, g], s_sem.at[k, g, le]
        )

    def pick_rows(k, g):
        if k in keeps:
            keeps.pop(k).wait()
        for at in range(4 * g, 4 * g + 4):
            remote(
                mine.at[k], blocks.at[k, at, other], p_send.at[k, at], p_recv.at[k, at], c=other
            ).wait_recv()
        chosen = pick_out[g] if k < 2 else pick_w[g]
        got = jnp.dot(
            chosen,
            blocks[k, 4 * g : 4 * g + 4].reshape(4 * NC * TOK, LANES),
            preferred_element_type=F32,
        ).astype(BF)
        out_y[k, g] = got.reshape(NY, LE, GROUP, LANES)
        for le in range(LE):
            go(y_piece(k, g, 2, le))
        for le in range(LE):
            go(y_piece(k, g, 1, le))
            go(y_piece(k, g, 3, le))
        for le in range(LE):
            go(x_piece(k, g, 0, le))
            own_piece(k, g, le).start()

    def y_step(k, g):
        for le in range(LE):
            y_piece(k, g, 2, le).wait_recv()
            go(relayed(k, g, le))
        for le in range(LE):
            y_piece(k, g, 1, le).wait_recv()
            go(x_piece(k, g, 1, le))
            y_piece(k, g, 3, le).wait_recv()
            go(x_piece(k, g, 3, le))

    def y_last(k, g):
        for le in range(LE):
            relayed(k, g, le).wait_recv()
            go(x_piece(k, g, 2, le))

    infos[0, c] = info[...]
    for at in range(NZ):
        if at:
            remote(info, infos.at[at, c], i_send.at[0, 0], i_recv.at[at, c], c=other).wait_recv()
        remote(info, infos.at[at, other], i_send.at[0, 0], i_recv.at[at, other], c=other).wait_recv()

    row = lax.broadcasted_iota(jnp.int32, (NY * LE, TOK), 0)
    expert = ((((y + row // LE) % NY * NZ + z) * NC + c) * LE + row % LE).astype(F32)
    before = (
        lax.broadcasted_iota(jnp.int32, (TOK, TOK), 0) < lax.broadcasted_iota(jnp.int32, (TOK, TOK), 1)
    ).astype(F32).astype(BF)
    hits, weights = [], []
    for at in range(NZ):
        for cc in range(NC):
            named = infos[at, cc].astype(F32)
            hit = jnp.zeros((NY * LE, TOK), F32)
            weight = jnp.zeros((NY * LE, TOK), F32)
            for k in range(8):
                same = named[k : k + 1] == expert
                hit = jnp.where(same, 1.0, hit)
                weight = jnp.where(same, named[8 + k : 9 + k], weight)
            hits.append(hit)
            weights.append(weight)
    ranks = jnp.dot(jnp.concatenate(hits, axis=0).astype(BF), before, preferred_element_type=F32)
    slot_row = lax.broadcasted_iota(jnp.int32, (GROUP, TOK), 0).astype(F32)
    for s in range(NZ * NC):
        g, i = s // 8, s % 8
        goal = jnp.where(
            hits[s] > 0, ranks[s * NY * LE : (s + 1) * NY * LE] + float(SLOTS * i), -1.0
        )
        for e in range(NY * LE):
            same = slot_row == goal[e : e + 1]
            at = (g, pl.ds(e * GROUP, GROUP), pl.ds(i * TOK, TOK))
            pick_out[at] = jnp.where(same, 1.0, 0.0).astype(BF)
            pick_w[at] = jnp.where(same, weights[s][e : e + 1], 0.0).astype(BF)

    for k in range(4):
        z_step(k, 1)
        if k:
            y_step(k - 1, 0)
        z_step(k, 2)
        if k < 3:
            keeps[k + 1] = start_chunk(k + 1)
        pick_rows(k, 0)
        z_step(k, 3)
        if k:
            y_last(k - 1, 0)
            y_step(k - 1, 1)
        z_step(k, 4)
        pick_rows(k, 1)
        if k:
            y_last(k - 1, 1)
    y_step(3, 0)
    y_last(3, 0)
    y_step(3, 1)
    y_last(3, 1)
    for k in range(4):
        for g in range(2):
            for le in range(LE):
                own_piece(k, g, le).wait()
                for d in range(NY):
                    slot = 4 * (k // 2) + 2 * (1 - h) + k % 2
                    there = rows.at[slot, le, (y + NY - d) % NY, g]
                    remote(
                        there, there, x_send.at[k, g, d, le], x_recv.at[k, g, d, le],
                        x=x_up if le == 0 else x_down,
                    ).wait_recv()
    for copy in waits:
        copy.wait_send()


def dispatch(mine, info):
    vmem = pl.BlockSpec(memory_space=pltpu.VMEM)
    anyw = pl.BlockSpec(memory_space=pl.ANY)
    dma = pltpu.SemaphoreType.DMA
    return pl.pallas_call(
        dispatch_kernel,
        out_shape=(
            jax.ShapeDtypeStruct((8, LE, NY, 2, GROUP, LANES), BF),
            jax.ShapeDtypeStruct((2, NY * LE * GROUP, 4 * NC * TOK), BF),
        ),
        in_specs=[vmem, vmem],
        out_specs=(anyw, vmem),
        scratch_shapes=[
            pltpu.VMEM((4, NZ, NC, TOK, LANES), BF),
            pltpu.VMEM((NZ, NC, 16, TOK), BF),
            pltpu.VMEM((2, NY * LE * GROUP, 4 * NC * TOK), BF),
            pltpu.VMEM((4, 2, NY, LE, GROUP, LANES), BF),
            pltpu.VMEM((4, 2, LE, GROUP, LANES), BF),
            dma((NZ, 2)), dma((NZ, NC)),
            dma((4, 7)), dma((4, 7)),
            dma((4, NZ)), dma((4, NZ)),
            dma((4, 2, 3, LE)), dma((4, 2, 3, LE)),
            dma((4, 2, LE)), dma((4, 2, LE)),
            dma((4, 2, NY, LE)), dma((4, 2, NY, LE)),
            dma((4,)), dma((4, 2, LE)),
        ],
        compiler_params=pltpu.CompilerParams(
            collective_id=0, has_side_effects=True, vmem_limit_bytes=48 << 20
        ),
        name="dispatch",
    )(mine, info)


def nt(a, b):
    return lax.dot_general(a, b, (((1,), (1,)), ((), ())), preferred_element_type=F32)


def tn(a, b):
    return lax.dot_general(a, b, (((0,), (0,)), ((), ())), preferred_element_type=F32)


def expert_kernel(rows, w_gate, w_up, w_down, g_gate, g_up, g_down, part, probs):
    def cut(q):
        return slice(q * LANES, (q + 1) * LANES)

    gate = sum(nt(rows[q, 0], w_gate[0, :, cut(q)]) for q in range(4))
    up = sum(nt(rows[q, 0], w_up[0, :, cut(q)]) for q in range(4))
    back = sum(nt(rows[4 + q, 0], w_down[0, :, cut(q)]) for q in range(4))
    sig = 1.0 / (1.0 + jnp.exp(-gate))
    act = gate * sig
    hidden = (act * up).astype(BF)
    d_gate = (back * up * sig * (1.0 + gate * (1.0 - sig))).astype(BF)
    d_up = (back * act).astype(BF)
    product = (hidden.astype(F32) * back).astype(BF)
    probs[0] = nt(jnp.ones((16, product.shape[1]), BF), product).astype(BF)
    for q in range(4):
        g_down[0, :, cut(q)] = tn(hidden, rows[4 + q, 0]).astype(BF)
        g_gate[0, :, cut(q)] = tn(d_gate, rows[q, 0]).astype(BF)
        g_up[0, :, cut(q)] = tn(d_up, rows[q, 0]).astype(BF)
        part[q, 0] = (
            jnp.dot(d_gate, w_gate[0, :, cut(q)], preferred_element_type=F32)
            + jnp.dot(d_up, w_up[0, :, cut(q)], preferred_element_type=F32)
        ).astype(BF)


def experts(rows, w_gate, w_up, w_down):
    le, hid, width = w_gate.shape
    n = rows.shape[2]
    weight = pl.BlockSpec((1, hid, width), lambda i: (i, 0, 0))
    return pl.pallas_call(
        expert_kernel,
        grid=(le,),
        out_shape=(
            jax.ShapeDtypeStruct((le, hid, width), BF),
            jax.ShapeDtypeStruct((le, hid, width), BF),
            jax.ShapeDtypeStruct((le, hid, width), BF),
            jax.ShapeDtypeStruct((4, le, n, LANES), BF),
            jax.ShapeDtypeStruct((le, 16, n), BF),
        ),
        in_specs=[pl.BlockSpec((8, 1, n, LANES), lambda i: (0, i, 0, 0)), weight, weight, weight],
        out_specs=(
            weight, weight, weight,
            pl.BlockSpec((4, 1, n, LANES), lambda i: (0, i, 0, 0)),
            pl.BlockSpec((1, 16, n), lambda i: (i, 0, 0)),
        ),
        compiler_params=pltpu.CompilerParams(vmem_limit_bytes=56 << 20),
        cost_estimate=pl.CostEstimate(flops=8_000_000_000, bytes_accessed=25_000_000, transcendentals=250_000),
        name="experts",
    )(rows, w_gate, w_up, w_down)


def dot(spec, a, b):
    return jnp.einsum(spec, a, b, preferred_element_type=F32)


def body(tokens, grad_out, routes, probs, w_gate, w_up, w_down):
    x = lax.axis_index("x")
    z = lax.axis_index("z")
    c = lax.axis_index("c")
    h = x % 2
    half = 2 * LANES
    quarter = LANES
    tok_rows = TOK
    le = LE
    cut = [
        lax.dynamic_slice_in_dim(a, h * half + q * LANES, LANES, axis=1)
        for a in (tokens, grad_out)
        for q in range(2)
    ]
    info = jnp.concatenate([routes.T.astype(BF), probs.T], axis=0)
    rows, pick = dispatch(jnp.stack(cut), info)
    g_gate, g_up, g_down, part, prob = experts(
        rows.reshape(8, LE, NY * 2 * GROUP, LANES), w_gate, w_up, w_down
    )
    up_ring = [(i, (i + 1) % NX) for i in range(NX)]
    down_ring = [(i, (i + NX - 1) % NX) for i in range(NX)]
    part = part.reshape(2, 2, LE, NY * 2 * GROUP, LANES)
    keep = jnp.where(h == 0, part[0], part[1])
    give = jnp.where(h == 0, part[1], part[0])
    got0 = lax.ppermute(give[:, 0], "x", up_ring)
    got1 = lax.ppermute(give[:, 1], "x", down_ring)
    kept = (keep.astype(F32) + jnp.stack([got0, got1], axis=1).astype(F32)).astype(BF)
    kept = kept.reshape(2, LE, NY, 2, GROUP, LANES)
    kept = lax.all_to_all(kept, "y", split_axis=2, concat_axis=2, tiled=True)
    y = lax.axis_index("y")
    kept = jnp.roll(kept, -y, axis=2)
    pr = prob[:, 0].reshape(LE, NY, 2, GROUP)
    pr = lax.all_to_all(pr, "y", split_axis=1, concat_axis=1, tiled=True)
    pr = jnp.roll(pr, -y, axis=1)
    pick6 = pick.reshape(2, NY, LE, GROUP, 4 * NC, TOK)
    home = dot("gyljst,qlygjd->gstqd", pick6, kept).astype(BF)
    home = home.reshape(NZ, NC, TOK, half)
    home = jnp.roll(jnp.stack([home[PLACE[r]] for r in range(NZ)]), z, axis=0).reshape(NZ * NC, TOK, half)
    home = lax.psum_scatter(home, ("z", "c"), scatter_dimension=0, tiled=False)
    ptok = dot("gyljst,lygj->gsylt", pick6, pr).astype(BF).reshape(NZ, NC, NY, LE, TOK)
    ptok = jnp.roll(jnp.roll(jnp.stack([ptok[PLACE[r]] for r in range(NZ)]), z, axis=0), y, axis=2).reshape(NZ * NC, NY * LE, TOK)
    ptok = lax.all_to_all(ptok, ("z", "c"), split_axis=0, concat_axis=0, tiled=True)
    ptok = lax.psum(ptok.astype(F32), "x")
    zeros = jnp.zeros_like(home)
    wide = jnp.where(h == 0, jnp.concatenate([home, zeros], -1), jnp.concatenate([zeros, home], -1))
    grad_tokens = lax.psum(wide, "x")
    by_expert = jnp.transpose(ptok.reshape(NZ * NC, NY, le, tok_rows), (1, 0, 2, 3)).reshape(-1, tok_rows)
    chosen = routes[:, :, None] == jnp.arange(by_expert.shape[0])[None, None, :]
    total = jnp.sum(jnp.where(chosen, by_expert.T[:, None, :], 0), axis=-1)
    grad_probs = (total / probs.astype(F32)).astype(BF)
    return (grad_tokens, grad_probs, g_gate, g_up, g_down)


def solution(mesh):
    cut = Mesh(mesh.devices.reshape(NY, NZ, NC, NX), ("y", "z", "c", "x"))
    rows = P(("y", "z", "c"), None)
    weights = P(("y", "z", "c"), "x", None)
    return jax.shard_map(
        body,
        mesh=cut,
        in_specs=(rows, rows, rows, rows, weights, weights, weights),
        out_specs=(rows, rows, weights, weights, weights),
        check_vma=False,
    )
```

```python
import functools

import jax
import jax.numpy as jnp
from jax import lax
from jax.experimental import pallas as pl
from jax.experimental.pallas import tpu as pltpu
from jax.sharding import Mesh, PartitionSpec as P

NY, NZ, NC, NX = 4, 8, 2, 4
SLOTS = 10
LE = 2
TOK = 128
GROUP = 4 * NC * SLOTS
LANES = 512
WIDE = 256
BF = jnp.bfloat16
F32 = jnp.float32
MESH = pl.DeviceIdType.MESH
PLACE = {0: 0, 1: 1, 7: 2, 2: 3, 6: 4, 3: 5, 5: 6, 4: 7}


def remote(src, dst, send, recv, **where):
    return pltpu.make_async_remote_copy(
        src_ref=src, dst_ref=dst, send_sem=send, recv_sem=recv, device_id=where, device_id_type=MESH
    )


def axes():
    return tuple(lax.axis_index(n) for n in ("y", "z", "c", "x"))


def dispatch_kernel(
    mine, info, rows, goals,
    blocks, infos, pick, pick_w, out_y, relay,
    i_send, i_recv, z_send, z_recv, p_send, p_recv, y_send, y_recv, r_send, r_recv, x_send, x_recv, l_sem, s_sem,
):
    y, z, c, x = axes()
    h = x % 2
    other = 1 - c
    sign = 1 - 2 * c
    z_long, z_short = (z + sign + NZ) % NZ, (z - sign + NZ) % NZ
    y_up, y_down = (y + 1) % NY, (y + NY - 1) % NY
    x_up, x_down = (x + 1) % NX, (x + NX - 1) % NX

    barrier = pltpu.get_barrier_semaphore()
    for m in range(NZ):
        for cc in ((c, other) if m else (other,)):
            pl.semaphore_signal(barrier, inc=1, device_id={"z": (z + m) % NZ, "c": cc}, device_id_type=MESH)
    for yy in (y_up, y_down):
        pl.semaphore_signal(barrier, inc=1, device_id={"y": yy}, device_id_type=MESH)
    for xx in (x_up, x_down):
        pl.semaphore_signal(barrier, inc=1, device_id={"x": xx}, device_id_type=MESH)
    pl.semaphore_wait(barrier, 2 * NZ - 1 + 4)

    waits = []

    def go(copy):
        copy.start()
        waits.append(copy)

    def info_copy(m, cc, far):
        at = PLACE[(NZ - m) % NZ]
        return remote(
            info, infos.at[at, c], i_send.at[m, far], i_recv.at[at, c], z=(z + m) % NZ, c=cc
        )

    for m in range(NZ):
        if m:
            go(info_copy(m, c, 0))
        go(info_copy(m, other, 1))

    def place(long, s):
        if s == 0:
            return 0
        if long:
            return 7 if s == 4 else 2 * s - c
        return 2 * s - 1 + c

    def hop(k, long, s):
        index = (s - 1) if long else (3 + s)
        src = mine.at[k] if s == 1 else blocks.at[k, place(long, s - 1), c]
        return remote(
            src, blocks.at[k, place(long, s), c], z_send.at[k, index], z_recv.at[k, index],
            z=z_long if long else z_short,
        )

    def to_partner(k, at):
        src = mine.at[k] if isinstance(at, int) and at == 0 else blocks.at[k, at, c]
        return remote(src, blocks.at[k, at, c], p_send.at[k, at], p_recv.at[k, at], c=other)

    def start_chunk(k):
        go(hop(k, True, 1))
        go(hop(k, False, 1))
        go(to_partner(k, 0))
        keep = pltpu.make_async_copy(mine.at[k], blocks.at[k, 0, c], l_sem.at[k])
        keep.start()
        return keep

    keeps = {0: start_chunk(0)}

    def z_step(k, s):
        for long in ((True, False) if s < 4 else (True,)):
            hop(k, long, s).wait_recv()
            if s < (4 if long else 3):
                go(hop(k, long, s + 1))
            go(to_partner(k, place(long, s)))

    def y_piece(k, g, d, le):
        src = out_y.at[k, g, d, le]
        slot = 4 * (k // 2) + 2 * h + k % 2
        landing = rows.at[slot, le, y, g]
        sems = dict(send=y_send.at[k, g, d - 1, le], recv=y_recv.at[k, g, d - 1, le])
        if d == 1:
            return remote(src, landing, y=y_up, **sems)
        if d == 3:
            return remote(src, landing, y=y_down, **sems)
        return remote(src, relay.at[k, g, le], y=y_up if le == 0 else y_down, **sems)

    def relayed(k, g, le):
        slot = 4 * (k // 2) + 2 * h + k % 2
        came = y_down if le == 0 else y_up
        return remote(
            relay.at[k, g, le], rows.at[slot, le, came, g], r_send.at[k, g, le], r_recv.at[k, g, le],
            y=y_up if le == 0 else y_down,
        )

    def x_piece(k, g, d, le):
        slot = 4 * (k // 2) + 2 * h + k % 2
        there = rows.at[slot, le, (y + NY - d) % NY, g]
        src = out_y.at[k, g, 0, le] if d == 0 else there
        return remote(
            src, there, x_send.at[k, g, d, le], x_recv.at[k, g, d, le], x=x_up if le == 0 else x_down
        )

    def own_piece(k, g, le):
        slot = 4 * (k // 2) + 2 * h + k % 2
        return pltpu.make_async_copy(
            out_y.at[k, g, 0, le], rows.at[slot, le, y, g], s_sem.at[k, g, le]
        )

    def pick_rows(k, g):
        if k in keeps:
            keeps.pop(k).wait()
        for at in range(4 * g, 4 * g + 4):
            remote(
                mine.at[k], blocks.at[k, at, other], p_send.at[k, at], p_recv.at[k, at], c=other
            ).wait_recv()
        chosen = pick[g] if k < 2 else pick_w[g]
        got = jnp.dot(
            chosen,
            blocks[k, 4 * g : 4 * g + 4].reshape(4 * NC * TOK, LANES),
            preferred_element_type=F32,
        ).astype(BF)
        out_y[k, g] = got.reshape(NY, LE, GROUP, LANES)
        for le in range(LE):
            go(y_piece(k, g, 2, le))
        for le in range(LE):
            go(y_piece(k, g, 1, le))
            go(y_piece(k, g, 3, le))
        for le in range(LE):
            go(x_piece(k, g, 0, le))
            own_piece(k, g, le).start()

    def y_step(k, g):
        for le in range(LE):
            y_piece(k, g, 2, le).wait_recv()
            go(relayed(k, g, le))
        for le in range(LE):
            y_piece(k, g, 1, le).wait_recv()
            go(x_piece(k, g, 1, le))
            y_piece(k, g, 3, le).wait_recv()
            go(x_piece(k, g, 3, le))

    def y_last(k, g):
        for le in range(LE):
            relayed(k, g, le).wait_recv()
            go(x_piece(k, g, 2, le))

    infos[0, c] = info[...]
    for at in range(NZ):
        if at:
            remote(info, infos.at[at, c], i_send.at[0, 0], i_recv.at[at, c], c=other).wait_recv()
        remote(info, infos.at[at, other], i_send.at[0, 0], i_recv.at[at, other], c=other).wait_recv()

    row = lax.broadcasted_iota(jnp.int32, (NY * LE, TOK), 0)
    expert = ((((y + row // LE) % NY * NZ + z) * NC + c) * LE + row % LE).astype(F32)
    before = (
        lax.broadcasted_iota(jnp.int32, (TOK, TOK), 0) < lax.broadcasted_iota(jnp.int32, (TOK, TOK), 1)
    ).astype(F32).astype(BF)
    hits, weights = [], []
    for at in range(NZ):
        for cc in range(NC):
            named = infos[at, cc].astype(F32)
            hit = jnp.zeros((NY * LE, TOK), F32)
            weight = jnp.zeros((NY * LE, TOK), F32)
            for k in range(8):
                same = named[k : k + 1] == expert
                hit = jnp.where(same, 1.0, hit)
                weight = jnp.where(same, named[8 + k : 9 + k], weight)
            hits.append(hit)
            weights.append(weight)
    ranks = jnp.dot(jnp.concatenate(hits, axis=0).astype(BF), before, preferred_element_type=F32)
    slot_row = lax.broadcasted_iota(jnp.int32, (GROUP, TOK), 0).astype(F32)
    for s in range(NZ * NC):
        g, i = s // 8, s % 8
        goal = jnp.where(
            hits[s] > 0, ranks[s * NY * LE : (s + 1) * NY * LE] + float(SLOTS * i), -1.0
        )
        goals[s] = goal
        for e in range(NY * LE):
            same = slot_row == goal[e : e + 1]
            at = (g, pl.ds(e * GROUP, GROUP), pl.ds(i * TOK, TOK))
            pick[at] = jnp.where(same, 1.0, 0.0).astype(BF)
            pick_w[at] = jnp.where(same, weights[s][e : e + 1], 0.0).astype(BF)

    for k in range(4):
        z_step(k, 1)
        if k:
            y_step(k - 1, 0)
        z_step(k, 2)
        if k < 3:
            keeps[k + 1] = start_chunk(k + 1)
        pick_rows(k, 0)
        z_step(k, 3)
        if k:
            y_last(k - 1, 0)
            y_step(k - 1, 1)
        z_step(k, 4)
        pick_rows(k, 1)
        if k:
            y_last(k - 1, 1)
    y_step(3, 0)
    y_last(3, 0)
    y_step(3, 1)
    y_last(3, 1)
    for k in range(4):
        for g in range(2):
            for le in range(LE):
                own_piece(k, g, le).wait()
                for d in range(NY):
                    slot = 4 * (k // 2) + 2 * (1 - h) + k % 2
                    there = rows.at[slot, le, (y + NY - d) % NY, g]
                    remote(
                        there, there, x_send.at[k, g, d, le], x_recv.at[k, g, d, le],
                        x=x_up if le == 0 else x_down,
                    ).wait_recv()
    for copy in waits:
        copy.wait_send()


def dispatch(mine, info):
    vmem = pl.BlockSpec(memory_space=pltpu.VMEM)
    anyw = pl.BlockSpec(memory_space=pl.ANY)
    dma = pltpu.SemaphoreType.DMA
    return pl.pallas_call(
        dispatch_kernel,
        out_shape=(
            jax.ShapeDtypeStruct((8, LE, NY, 2, GROUP, LANES), BF),
            jax.ShapeDtypeStruct((NZ * NC, NY * LE, TOK), F32),
        ),
        in_specs=[vmem, vmem],
        out_specs=(anyw, vmem),
        scratch_shapes=[
            pltpu.VMEM((4, NZ, NC, TOK, LANES), BF),
            pltpu.VMEM((NZ, NC, 16, TOK), BF),
            pltpu.VMEM((2, NY * LE * GROUP, 4 * NC * TOK), BF),
            pltpu.VMEM((2, NY * LE * GROUP, 4 * NC * TOK), BF),
            pltpu.VMEM((4, 2, NY, LE, GROUP, LANES), BF),
            pltpu.VMEM((4, 2, LE, GROUP, LANES), BF),
            dma((NZ, 2)), dma((NZ, NC)),
            dma((4, 7)), dma((4, 7)),
            dma((4, NZ)), dma((4, NZ)),
            dma((4, 2, 3, LE)), dma((4, 2, 3, LE)),
            dma((4, 2, LE)), dma((4, 2, LE)),
            dma((4, 2, NY, LE)), dma((4, 2, NY, LE)),
            dma((4,)), dma((4, 2, LE)),
        ],
        compiler_params=pltpu.CompilerParams(
            collective_id=0, has_side_effects=True, vmem_limit_bytes=48 << 20
        ),
        name="dispatch",
    )(mine, info)


def nt(a, b):
    return lax.dot_general(a, b, (((1,), (1,)), ((), ())), preferred_element_type=F32)


def tn(a, b):
    return lax.dot_general(a, b, (((0,), (0,)), ((), ())), preferred_element_type=F32)


def expert_kernel(rows, w_gate, w_up, w_down, g_gate, g_up, g_down, part, probs):
    def cut(q):
        return slice(q * LANES, (q + 1) * LANES)

    gate = sum(nt(rows[q, 0], w_gate[0, :, cut(q)]) for q in range(4))
    up = sum(nt(rows[q, 0], w_up[0, :, cut(q)]) for q in range(4))
    back = sum(nt(rows[4 + q, 0], w_down[0, :, cut(q)]) for q in range(4))
    sig = 1.0 / (1.0 + jnp.exp(-gate))
    act = gate * sig
    hidden = (act * up).astype(BF)
    d_gate = (back * up * sig * (1.0 + gate * (1.0 - sig))).astype(BF)
    d_up = (back * act).astype(BF)
    product = (hidden.astype(F32) * back).astype(BF)
    ones = jnp.ones((16, product.shape[1]), BF)
    probs[...] = jnp.zeros_like(probs)
    for yy in range(NY):
        for g in range(2):
            at = (2 * yy + g) * GROUP
            probs[0, yy, g, :, 0:GROUP] = nt(ones, product[at : at + GROUP]).astype(BF)
    for q in range(4):
        g_down[0, :, cut(q)] = tn(hidden, rows[4 + q, 0]).astype(BF)
        g_gate[0, :, cut(q)] = tn(d_gate, rows[q, 0]).astype(BF)
        g_up[0, :, cut(q)] = tn(d_up, rows[q, 0]).astype(BF)
        sent = (
            jnp.dot(d_gate, w_gate[0, :, cut(q)], preferred_element_type=F32)
            + jnp.dot(d_up, w_up[0, :, cut(q)], preferred_element_type=F32)
        ).astype(BF)
        part[2 * q, 0] = sent[:, :WIDE]
        part[2 * q + 1, 0] = sent[:, WIDE:]


def experts(rows, w_gate, w_up, w_down):
    le, hid, width = w_gate.shape
    n = rows.shape[2]
    weight = pl.BlockSpec((1, hid, width), lambda i: (i, 0, 0))
    return pl.pallas_call(
        expert_kernel,
        grid=(le,),
        out_shape=(
            jax.ShapeDtypeStruct((le, hid, width), BF),
            jax.ShapeDtypeStruct((le, hid, width), BF),
            jax.ShapeDtypeStruct((le, hid, width), BF),
            jax.ShapeDtypeStruct((8, le, n, WIDE), BF),
            jax.ShapeDtypeStruct((le, NY, 2, 16, TOK), BF),
        ),
        in_specs=[pl.BlockSpec((8, 1, n, LANES), lambda i: (0, i, 0, 0)), weight, weight, weight],
        out_specs=(
            weight, weight, weight,
            pl.BlockSpec((8, 1, n, WIDE), lambda i: (0, i, 0, 0)),
            pl.BlockSpec((1, NY, 2, 16, TOK), lambda i: (i, 0, 0, 0, 0)),
        ),
        compiler_params=pltpu.CompilerParams(vmem_limit_bytes=56 << 20),
        cost_estimate=pl.CostEstimate(flops=8_000_000_000, bytes_accessed=25_000_000, transcendentals=250_000),
        name="experts",
    )(rows, w_gate, w_up, w_down)


def return_kernel(
    part, probs, goals, info, grads, grad_probs,
    own, x_in, kept, y_in, relay, pick, pick_t, sums, p_in, z_out, z_in, f_out, f_in, v_out, v_in, b_in, b_all, b_out,
    o_sem, x_send, x_recv, y_send, y_recv, r_send, r_recv, p_send, p_recv, z_send, z_recv, f_send, f_recv,
    b_send, b_recv, v_send, v_recv, g_send, g_recv,
):
    y, z, c, x = axes()
    h = x % 2
    other = 1 - c
    sign = 1 - 2 * c
    z_long, z_short = (z + sign + NZ) % NZ, (z - sign + NZ) % NZ
    y_up, y_down = (y + 1) % NY, (y + NY - 1) % NY
    x_up, x_down = (x + 1) % NX, (x + NX - 1) % NX
    x_far = (x + 2) % NX

    barrier = pltpu.get_barrier_semaphore()
    for m in range(NZ):
        for cc in ((c, other) if m else (other,)):
            pl.semaphore_signal(barrier, inc=1, device_id={"z": (z + m) % NZ, "c": cc}, device_id_type=MESH)
    for m in range(1, NY):
        pl.semaphore_signal(barrier, inc=1, device_id={"y": (y + m) % NY}, device_id_type=MESH)
    for m in range(1, NX):
        pl.semaphore_signal(barrier, inc=1, device_id={"x": (x + m) % NX}, device_id_type=MESH)
    pl.semaphore_wait(barrier, 2 * NZ - 1 + NY - 1 + NX - 1)

    waits = []

    def go(copy):
        copy.start()
        waits.append(copy)

    def x_copy(j, le):
        return remote(
            part.at[4 * (1 - h) + j, le], x_in.at[j, le], x_send.at[j, le], x_recv.at[j, le],
            x=x_up if le == 0 else x_down,
        )

    def own_copy(j):
        return pltpu.make_async_copy(part.at[4 * h + j], own.at[j], o_sem.at[j])

    def b_copy(m):
        return remote(
            probs.at[:, (y + NY - m) % NY], b_in.at[m], b_send.at[m], b_recv.at[m], y=(y + NY - m) % NY
        )

    for m in range(1, NY):
        go(b_copy(m))
    for j in range(4):
        for le in range(LE):
            go(x_copy(j, le))
        own_copy(j).start()
    b_own = pltpu.make_async_copy(probs.at[:, y], b_in.at[0], b_send.at[0])
    b_own.start()

    slot_row = lax.broadcasted_iota(jnp.int32, (GROUP, TOK), 0).astype(F32)
    same_lane = (
        lax.broadcasted_iota(jnp.int32, (TOK, TOK), 0) == lax.broadcasted_iota(jnp.int32, (TOK, TOK), 1)
    ).astype(F32).astype(BF)
    for s in range(NZ * NC):
        g, i = s // 8, s % 8
        goal = goals[s]
        for e in range(NY * LE):
            pick[g, pl.ds(e * GROUP, GROUP), pl.ds(i * TOK, TOK)] = jnp.where(
                slot_row == goal[e : e + 1], 1.0, 0.0
            ).astype(BF)
        pick_t[g, pl.ds(i * TOK, TOK), :] = nt(same_lane, pick[g, :, pl.ds(i * TOK, TOK)]).astype(BF)

    def v_copy(at, r, cc, far):
        back = PLACE[(NZ - r) % NZ]
        return remote(
            v_out.at[at, cc], v_in.at[back, c], v_send.at[at, far], v_recv.at[back, c], z=(z + r) % NZ, c=cc
        )

    b_own.wait()
    for m in range(1, NY):
        b_copy(m).wait_recv()
    lane_row = lax.broadcasted_iota(jnp.int32, (16, 4 * NC * TOK), 0)
    for g in range(2):
        values = jnp.zeros((16, 4 * NC * TOK), F32)
        for e in range(NY * LE):
            got = jnp.dot(
                b_in[e // LE, e % LE, g][:, :GROUP],
                pick[g, pl.ds(e * GROUP, GROUP), :],
                preferred_element_type=F32,
            )
            values = jnp.where(lane_row == e, got, values)
        values = values.astype(BF)
        for i in range(8):
            v_out[4 * g + i // 2, i % 2] = values[:, i * TOK : (i + 1) * TOK]
    for r in range(NZ):
        if r:
            go(v_copy(PLACE[r], r, c, 0))
        go(v_copy(PLACE[r], r, other, 1))

    def y_copy(j, d, le):
        src = kept.at[j, le, (y + NY - d) % NY]
        sems = dict(send=y_send.at[j, d - 1, le], recv=y_recv.at[j, d - 1, le])
        if d == 1:
            return remote(src, y_in.at[j, :, 1, le], y=y_down, **sems)
        if d == 3:
            return remote(src, y_in.at[j, :, 3, le], y=y_up, **sems)
        return remote(src, relay.at[j, le], y=y_up if le == 0 else y_down, **sems)

    def relayed(j, le):
        return remote(
            relay.at[j, le], y_in.at[j, :, 2, le], r_send.at[j, le], r_recv.at[j, le],
            y=y_up if le == 0 else y_down,
        )

    def x_stage(j):
        own_copy(j).wait()
        for le in range(LE):
            x_copy(j, le).wait_recv()
            kept[j, le] = (own[j, le].astype(F32) + x_in[j, le].astype(F32)).astype(BF)
            go(y_copy(j, 2, le))
            go(y_copy(j, 1, le))
            go(y_copy(j, 3, le))
            y_in[j, :, 0, le] = kept[j, le, y]

    def relay_stage(j):
        for le in range(LE):
            y_copy(j, 2, le).wait_recv()
            go(relayed(j, le))

    def p_copy(j, g):
        return remote(
            sums.at[j, g, other], p_in.at[j, g], p_send.at[j, g], p_recv.at[j, g], c=other
        )

    def sum_stage(j):
        for le in range(LE):
            y_copy(j, 1, le).wait_recv()
            y_copy(j, 3, le).wait_recv()
            relayed(j, le).wait_recv()
        for g in (1, 0):
            got = jnp.dot(
                pick_t[g], y_in[j, g].reshape(NY * LE * GROUP, WIDE), preferred_element_type=F32
            ).astype(BF).reshape(4, NC, TOK, WIDE)
            for cc in range(NC):
                sums[j, g, cc] = got[:, cc]
            go(p_copy(j, g))

    def place(long, s):
        if s == 0:
            return 0
        if long:
            return 7 if s == 4 else 2 * s - c
        return 2 * s - 1 + c

    def z_copy(j, long, s):
        index = (s - 1) if long else (3 + s)
        return remote(
            z_out.at[j, index], z_in.at[j, index], z_send.at[j, index], z_recv.at[j, index],
            z=z_short if long else z_long,
        )

    def both(j, at):
        g, i = (0, 0) if isinstance(at, int) and at == 0 else (at // 4, at % 4)
        return sums[j, g, c, i].astype(F32) + p_in[j, g, i].astype(F32)

    def z_stage(j, s):
        if s == 4:
            for g in range(2):
                p_copy(j, g).wait_recv()
        for long in ((True, False) if s < 4 else (True,)):
            index = (s - 1) if long else (3 + s)
            total = both(j, place(long, s))
            if s < (4 if long else 3):
                z_copy(j, long, s + 1).wait_recv()
                total = total + z_in[j, index + 1].astype(F32)
            z_out[j, index] = total.astype(BF)
            go(z_copy(j, long, s))

    def f_copy(j, m):
        return remote(
            f_out.at[j], f_in.at[j, m - 1], f_send.at[j, m - 1], f_recv.at[j, m - 1], x=(x + m) % NX
        )

    def home_stage(j):
        total = both(j, 0)
        for long in (True, False):
            z_copy(j, long, 1).wait_recv()
            total = total + z_in[j, 0 if long else 4].astype(F32)
        f_out[j] = total.astype(BF)
        for m in (2, 1, 3):
            go(f_copy(j, m))

    def end_stage(j):
        for m in (1, 3, 2):
            f_copy(j, m).wait_recv()
        grads[4 * (1 - h) + j] = (f_in[j, 0].astype(F32) + f_in[j, 2].astype(F32)).astype(BF)
        grads[4 * h + j] = (f_out[j].astype(F32) + f_in[j, 1].astype(F32)).astype(BF)

    def g_copy(m):
        return remote(b_out, b_all.at[x], g_send.at[m], g_recv.at[x], x=(x + m) % NX)

    def gate_stage():
        for at in range(NZ):
            for far, cc in ((0, c), (1, other)):
                if at == 0 and far == 0:
                    continue
                remote(
                    v_out.at[at, cc], v_in.at[at, cc], v_send.at[at, far], v_recv.at[at, cc], c=other
                ).wait_recv()
        v_in[0, c] = v_out[0, c]
        row = lax.broadcasted_iota(jnp.int32, (16, TOK), 0)
        base = (y + row // LE) % NY * (NZ * NC * LE) + row % LE
        base = jnp.where(row < NY * LE, base, -NZ * NC * LE)
        found = [jnp.zeros((16, TOK), F32) for _ in range(8)]
        for r in range(NZ):
            for cc in range(NC):
                expert = (base + ((z + r) % NZ * NC + cc) * LE).astype(F32)
                value = v_in[PLACE[r], cc].astype(F32)
                for k in range(8):
                    same = info[k : k + 1].astype(F32) == expert
                    found[k] = jnp.where(same, value, found[k])
        for k in range(8):
            total = jnp.sum(found[k], axis=0, keepdims=True)
            b_out[k : k + 1] = total.astype(BF)
            b_out[8 + k : 9 + k] = total.astype(BF)
        for m in range(1, NX):
            go(g_copy(m))

    events = []
    for j in range(4):
        events += [(2 * j, j, x_stage, (j,)), (2 * j + 1, j, relay_stage, (j,)), (2 * j + 2, j, sum_stage, (j,))]
        events += [(2 * j + 3 + (4 - s), j, z_stage, (j, s)) for s in (4, 3, 2, 1)]
        events += [(2 * j + 7, j, home_stage, (j,)), (2 * j + 9, j, end_stage, (j,))]
    events.append((7.5, 0, gate_stage, ()))
    for _, _, stage, given in sorted(events, key=lambda e: (e[0], e[1])):
        stage(*given)
    b_all[x] = b_out[...]
    for m in range(1, NX):
        at = (x + NX - m) % NX
        remote(b_out, b_all.at[at], g_send.at[m], g_recv.at[at], x=x_up).wait_recv()
    total = (
        b_all[0].astype(F32) + b_all[1].astype(F32) + b_all[2].astype(F32) + b_all[3].astype(F32)
    )
    grad_probs[...] = total[:8] / info[...].astype(F32)[8:]
    for copy in waits:
        copy.wait_send()


def give_back(part, probs, goals, info):
    vmem = pl.BlockSpec(memory_space=pltpu.VMEM)
    anyw = pl.BlockSpec(memory_space=pl.ANY)
    dma = pltpu.SemaphoreType.DMA
    return pl.pallas_call(
        return_kernel,
        out_shape=(
            jax.ShapeDtypeStruct((8, TOK, WIDE), BF),
            jax.ShapeDtypeStruct((8, TOK), F32),
        ),
        in_specs=[anyw, vmem, vmem, vmem],
        out_specs=(vmem, vmem),
        scratch_shapes=[
            pltpu.VMEM((4, LE, NY, 2, GROUP, WIDE), BF),
            pltpu.VMEM((4, LE, NY, 2, GROUP, WIDE), BF),
            pltpu.VMEM((4, LE, NY, 2, GROUP, WIDE), BF),
            pltpu.VMEM((4, 2, NY, LE, GROUP, WIDE), BF),
            pltpu.VMEM((4, LE, 2, GROUP, WIDE), BF),
            pltpu.VMEM((2, NY * LE * GROUP, 4 * NC * TOK), BF),
            pltpu.VMEM((2, 4 * NC * TOK, NY * LE * GROUP), BF),
            pltpu.VMEM((4, 2, NC, 4, TOK, WIDE), BF),
            pltpu.VMEM((4, 2, 4, TOK, WIDE), BF),
            pltpu.VMEM((4, 7, TOK, WIDE), BF),
            pltpu.VMEM((4, 7, TOK, WIDE), BF),
            pltpu.VMEM((4, TOK, WIDE), BF),
            pltpu.VMEM((4, 3, TOK, WIDE), BF),
            pltpu.VMEM((NZ, NC, 16, TOK), BF),
            pltpu.VMEM((NZ, NC, 16, TOK), BF),
            pltpu.VMEM((NY, LE, 2, 16, TOK), BF),
            pltpu.VMEM((NX, 16, TOK), BF),
            pltpu.VMEM((16, TOK), BF),
            dma((4,)),
            dma((4, LE)), dma((4, LE)),
            dma((4, 3, LE)), dma((4, 3, LE)),
            dma((4, LE)), dma((4, LE)),
            dma((4, 2)), dma((4, 2)),
            dma((4, 7)), dma((4, 7)),
            dma((4, 3)), dma((4, 3)),
            dma((NY,)), dma((NY,)),
            dma((NZ, 2)), dma((NZ, NC)),
            dma((NX,)), dma((NX,)),
        ],
        compiler_params=pltpu.CompilerParams(
            collective_id=1, has_side_effects=True, vmem_limit_bytes=48 << 20
        ),
        name="give_back",
    )(part, probs, goals, info)


def body(tokens, grad_out, routes, probs, w_gate, w_up, w_down):
    h = lax.axis_index("x") % 2
    mine = jnp.stack(
        [
            lax.dynamic_slice_in_dim(a, h * 2 * LANES + q * LANES, LANES, axis=1)
            for a in (tokens, grad_out)
            for q in range(2)
        ]
    )
    info = jnp.concatenate([routes.T.astype(BF), probs.T], axis=0)
    rows, goals = dispatch(mine, info)
    g_gate, g_up, g_down, part, prob = experts(
        rows.reshape(8, LE, NY * 2 * GROUP, LANES), w_gate, w_up, w_down
    )
    grads, grad_probs = give_back(
        part.reshape(8, LE, NY, 2, GROUP, WIDE), prob, goals, info
    )
    grad_tokens = jnp.transpose(grads, (1, 0, 2)).reshape(tokens.shape)
    return (grad_tokens, grad_probs.T.astype(BF), g_gate, g_up, g_down)


def solution(mesh):
    cut = Mesh(mesh.devices.reshape(NY, NZ, NC, NX), ("y", "z", "c", "x"))
    rows = P(("y", "z", "c"), None)
    weights = P(("y", "z", "c"), "x", None)
    return jax.shard_map(
        body,
        mesh=cut,
        in_specs=(rows, rows, rows, rows, weights, weights, weights),
        out_specs=(rows, rows, weights, weights, weights),
        check_vma=False,
    )
```

```python
import jax
import jax.numpy as jnp
from jax import lax
from jax.experimental import pallas as pl
from jax.experimental.pallas import tpu as pltpu
from jax.sharding import Mesh, PartitionSpec as P

NY, NZ, NC, NX = 4, 8, 2, 4
SLOTS = 10
LE = 2
TOK = 128
GROUP = 4 * NC * SLOTS
LANES = 512
WIDE = 256
BF = jnp.bfloat16
F32 = jnp.float32
MESH = pl.DeviceIdType.MESH
PLACE = {0: 0, 1: 1, 7: 2, 2: 3, 6: 4, 3: 5, 5: 6, 4: 7}


def remote(src, dst, send, recv, **where):
    return pltpu.make_async_remote_copy(
        src_ref=src, dst_ref=dst, send_sem=send, recv_sem=recv, device_id=where, device_id_type=MESH
    )


def nt(a, b):
    return lax.dot_general(a, b, (((1,), (1,)), ((), ())), preferred_element_type=F32)


def axes():
    return tuple(lax.axis_index(n) for n in ("y", "z", "c", "x"))


def dispatch_kernel(
    mine, info, w_gate, w_up, w_down, rows_out, pick_out, pick_t_out, inner, probs,
    rows, held, acc, blocks, infos, pick, pick_t, pick_w, out_y, relay,
    i_send, i_recv, z_send, z_recv, p_send, p_recv, y_send, y_recv, r_send, r_recv, x_send, x_recv, l_sem, w_sem, o_sem, t_sem,
):
    y, z, c, x = axes()
    h = x % 2
    other = 1 - c
    sign = 1 - 2 * c
    z_long, z_short = (z + sign + NZ) % NZ, (z - sign + NZ) % NZ
    y_up, y_down = (y + 1) % NY, (y + NY - 1) % NY
    x_up, x_down = (x + 1) % NX, (x + NX - 1) % NX

    barrier = pltpu.get_barrier_semaphore()
    for m in range(NZ):
        for cc in ((c, other) if m else (other,)):
            pl.semaphore_signal(barrier, inc=1, device_id={"z": (z + m) % NZ, "c": cc}, device_id_type=MESH)
    for yy in (y_up, y_down):
        pl.semaphore_signal(barrier, inc=1, device_id={"y": yy}, device_id_type=MESH)
    for xx in (x_up, x_down):
        pl.semaphore_signal(barrier, inc=1, device_id={"x": xx}, device_id_type=MESH)
    loads = [
        pltpu.make_async_copy(w.at[le, :, pl.ds(q * LANES, LANES)], held.at[i, le, q], w_sem.at[i, le, q])
        for i, w in enumerate((w_gate, w_up, w_down))
        for le in range(LE)
        for q in range(4)
    ]
    for copy in loads:
        copy.start()
    pick[...] = jnp.zeros_like(pick)
    pick_w[...] = jnp.zeros_like(pick_w)
    acc[...] = jnp.zeros_like(acc)
    pl.semaphore_wait(barrier, 2 * NZ - 1 + 4)

    waits = []

    def go(copy):
        copy.start()
        waits.append(copy)

    def info_copy(m, cc, far):
        at = PLACE[(NZ - m) % NZ]
        return remote(
            info, infos.at[at, c], i_send.at[m, far], i_recv.at[at, c], z=(z + m) % NZ, c=cc
        )

    for m in range(NZ):
        if m:
            go(info_copy(m, c, 0))
        go(info_copy(m, other, 1))

    def place(long, s):
        if s == 0:
            return 0
        if long:
            return 7 if s == 4 else 2 * s - c
        return 2 * s - 1 + c

    def hop(k, long, s):
        index = (s - 1) if long else (3 + s)
        src = mine.at[k] if s == 1 else blocks.at[k, place(long, s - 1), c]
        return remote(
            src, blocks.at[k, place(long, s), c], z_send.at[k, index], z_recv.at[k, index],
            z=z_long if long else z_short,
        )

    def to_partner(k, at):
        src = mine.at[k] if isinstance(at, int) and at == 0 else blocks.at[k, at, c]
        return remote(src, blocks.at[k, at, c], p_send.at[k, at], p_recv.at[k, at], c=other)

    def start_chunk(k):
        go(hop(k, True, 1))
        go(hop(k, False, 1))
        go(to_partner(k, 0))
        keep = pltpu.make_async_copy(mine.at[k], blocks.at[k, 0, c], l_sem.at[k])
        keep.start()
        return keep

    keeps = {0: start_chunk(0)}

    def z_step(k, s):
        for long in ((True, False) if s < 4 else (True,)):
            hop(k, long, s).wait_recv()
            if s < (4 if long else 3):
                go(hop(k, long, s + 1))
            go(to_partner(k, place(long, s)))

    def y_piece(k, g, d, le):
        src = out_y.at[k, g, d, le]
        slot = 4 * (k // 2) + 2 * h + k % 2
        landing = rows.at[slot, le, y, g]
        sems = dict(send=y_send.at[k, g, d - 1, le], recv=y_recv.at[k, g, d - 1, le])
        if d == 1:
            return remote(src, landing, y=y_up, **sems)
        if d == 3:
            return remote(src, landing, y=y_down, **sems)
        return remote(src, relay.at[k, g, le], y=y_up if le == 0 else y_down, **sems)

    def relayed(k, g, le):
        slot = 4 * (k // 2) + 2 * h + k % 2
        came = y_down if le == 0 else y_up
        return remote(
            relay.at[k, g, le], rows.at[slot, le, came, g], r_send.at[k, g, le], r_recv.at[k, g, le],
            y=y_up if le == 0 else y_down,
        )

    def x_piece(k, g, d, le):
        slot = 4 * (k // 2) + 2 * h + k % 2
        there = rows.at[slot, le, (y + NY - d) % NY, g]
        src = out_y.at[k, g, 0, le] if d == 0 else there
        return remote(
            src, there, x_send.at[k, g, d, le], x_recv.at[k, g, d, le], x=x_up if le == 0 else x_down
        )

    def slot_of(k, half):
        return 4 * (k // 2) + 2 * half + k % 2

    def absorb(k, half):
        quarter = 2 * half + k % 2
        slot = slot_of(k, half)
        for le in range(LE):
            some = rows[slot, le].reshape(NY * 2 * GROUP, LANES)
            for i in (0, 1) if k < 2 else (2,):
                acc[le, i] += nt(some, held[i, le, quarter])
        pltpu.make_async_copy(rows.at[slot], rows_out.at[slot], o_sem.at[slot]).start()

    def x_landed(k):
        for g in range(2):
            for le in range(LE):
                for d in range(NY):
                    there = rows.at[slot_of(k, 1 - h), le, (y + NY - d) % NY, g]
                    remote(
                        there, there, x_send.at[k, g, d, le], x_recv.at[k, g, d, le],
                        x=x_up if le == 0 else x_down,
                    ).wait_recv()

    def activate():
        for le in range(LE):
            gate, up = acc[le, 0], acc[le, 1]
            sig = 1.0 / (1.0 + jnp.exp(-gate))
            act = gate * sig
            inner[le, 0] = (act * up).astype(BF)
            acc[le, 0] = up * sig * (1.0 + gate * (1.0 - sig))
            acc[le, 1] = act

    def finish():
        probs[...] = jnp.zeros_like(probs)
        ones = jnp.ones((16, acc.shape[3]), BF)
        for le in range(LE):
            back = acc[le, 2]
            inner[le, 1] = (back * acc[le, 0]).astype(BF)
            inner[le, 2] = (back * acc[le, 1]).astype(BF)
            product = (inner[le, 0].astype(F32) * back).astype(BF)
            for yy in range(NY):
                for g in range(2):
                    at = (2 * yy + g) * GROUP
                    probs[le, yy, g, :, 0:GROUP] = nt(ones, product[at : at + GROUP]).astype(BF)

    def pick_rows(k, g):
        if k in keeps:
            keeps.pop(k).wait()
        for at in range(4 * g, 4 * g + 4):
            remote(
                mine.at[k], blocks.at[k, at, other], p_send.at[k, at], p_recv.at[k, at], c=other
            ).wait_recv()
        chosen = pick[g] if k < 2 else pick_w[g]
        got = jnp.dot(
            chosen,
            blocks[k, 4 * g : 4 * g + 4].reshape(4 * NC * TOK, LANES),
            preferred_element_type=F32,
        ).astype(BF)
        out_y[k, g] = got.reshape(NY, LE, GROUP, LANES)
        for le in range(LE):
            go(y_piece(k, g, 2, le))
        for le in range(LE):
            go(y_piece(k, g, 1, le))
            go(y_piece(k, g, 3, le))
        for le in range(LE):
            go(x_piece(k, g, 0, le))
        for le in range(LE):
            rows[slot_of(k, h), le, y, g] = out_y[k, g, 0, le]

    def y_step(k, g):
        for le in range(LE):
            y_piece(k, g, 2, le).wait_recv()
            go(relayed(k, g, le))
        for le in range(LE):
            y_piece(k, g, 1, le).wait_recv()
            go(x_piece(k, g, 1, le))
            y_piece(k, g, 3, le).wait_recv()
            go(x_piece(k, g, 3, le))

    def y_last(k, g):
        for le in range(LE):
            relayed(k, g, le).wait_recv()
            go(x_piece(k, g, 2, le))

    infos[0, c] = info[...]
    for at in range(NZ):
        if at:
            remote(info, infos.at[at, c], i_send.at[0, 0], i_recv.at[at, c], c=other).wait_recv()
        remote(info, infos.at[at, other], i_send.at[0, 0], i_recv.at[at, other], c=other).wait_recv()

    row = lax.broadcasted_iota(jnp.int32, (NY * LE, TOK), 0)
    expert = ((((y + row // LE) % NY * NZ + z) * NC + c) * LE + row % LE).astype(F32)
    before = (
        lax.broadcasted_iota(jnp.int32, (TOK, TOK), 0) < lax.broadcasted_iota(jnp.int32, (TOK, TOK), 1)
    ).astype(F32).astype(BF)
    hits, weights = [], []
    for at in range(NZ):
        for cc in range(NC):
            named = infos[at, cc].astype(F32)
            hit = jnp.zeros((NY * LE, TOK), F32)
            weight = jnp.zeros((NY * LE, TOK), F32)
            for k in range(8):
                same = named[k : k + 1] == expert
                hit = jnp.where(same, 1.0, hit)
                weight = jnp.where(same, named[8 + k : 9 + k], weight)
            hits.append(hit)
            weights.append(weight)
    ranks = jnp.dot(jnp.concatenate(hits, axis=0).astype(BF), before, preferred_element_type=F32)
    slot_row = lax.broadcasted_iota(jnp.int32, (16, TOK), 0).astype(F32)
    for s in range(NZ * NC):
        g, i = s // 8, s % 8
        first, last = SLOTS * i // 16, (SLOTS * i + SLOTS - 1) // 16
        goal = jnp.where(
            hits[s] > 0, ranks[s * NY * LE : (s + 1) * NY * LE] + float(SLOTS * i), -1.0
        )
        for e in range(NY * LE):
            for tile in range(first, last + 1):
                same = slot_row == goal[e : e + 1] - float(16 * tile)
                at = (g, pl.ds(e * GROUP + 16 * tile, 16), pl.ds(i * TOK, TOK))
                pick[at] = jnp.where(same, 1.0, 0.0).astype(BF)
                pick_w[at] = jnp.where(same, weights[s][e : e + 1], 0.0).astype(BF)

    def pick_copies():
        return [
            pltpu.make_async_copy(pick, pick_out, t_sem.at[0]),
            pltpu.make_async_copy(pick_t, pick_t_out, t_sem.at[1]),
        ]

    def turn(g):
        same_lane = (
            lax.broadcasted_iota(jnp.int32, (TOK, TOK), 0) == lax.broadcasted_iota(jnp.int32, (TOK, TOK), 1)
        ).astype(F32).astype(BF)
        for i in range(8):
            at = pl.ds(i * TOK, TOK)
            pick_t[g, at, :] = nt(same_lane, pick[g, :, at]).astype(BF)
        if g:
            for copy in pick_copies():
                copy.start()

    def begin(k):
        keeps[k] = start_chunk(k)

    def ready():
        for copy in loads:
            copy.wait()

    def other_half(k):
        x_landed(k)
        absorb(k, 1 - h)

    events = [(16.0, ready, ()), (16.1, turn, (0,)), (21.0, turn, (1,))]
    for k in range(4):
        events += [(10 * k + 5 * n - 2, z_step, (k, n)) for n in (1, 2, 3, 4)]
        events += [(10 * k + 8.5, pick_rows, (k, 0)), (10 * k + 18.5, pick_rows, (k, 1))]
        if k:
            events.append((10 * k - 1.9, begin, (k,)))
        for g in range(2):
            n = 2 * k + g
            events += [(15 + 7.5 * n, y_step, (k, g)), (18.2 + 7.5 * n, y_last, (k, g))]
        end = 18.2 + 7.5 * (2 * k + 1)
        events += [(end + 0.1, absorb, (k, h)), (end + 6, other_half, (k,))]
    events.append((18.2 + 7.5 * 3 + 6.1, activate, ()))
    for _, stage, given in sorted(events, key=lambda e: e[0]):
        stage(*given)
    finish()
    for slot in range(8):
        pltpu.make_async_copy(rows.at[slot], rows_out.at[slot], o_sem.at[slot]).wait()
    for copy in pick_copies():
        copy.wait()
    for copy in waits:
        copy.wait_send()


def dispatch(mine, info, w_gate, w_up, w_down):
    hid = w_gate.shape[1]
    count = NY * 2 * GROUP
    vmem = pl.BlockSpec(memory_space=pltpu.VMEM)
    anyw = pl.BlockSpec(memory_space=pl.ANY)
    dma = pltpu.SemaphoreType.DMA
    return pl.pallas_call(
        dispatch_kernel,
        out_shape=(
            jax.ShapeDtypeStruct((8, LE, NY, 2, GROUP, LANES), BF),
            jax.ShapeDtypeStruct((2, NY * LE * GROUP, 4 * NC * TOK), BF),
            jax.ShapeDtypeStruct((2, 4 * NC * TOK, NY * LE * GROUP), BF),
            jax.ShapeDtypeStruct((LE, 3, count, hid), BF),
            jax.ShapeDtypeStruct((LE, NY, 2, 16, TOK), BF),
        ),
        in_specs=[vmem, vmem, anyw, anyw, anyw],
        out_specs=(anyw, anyw, anyw, vmem, vmem),
        scratch_shapes=[
            pltpu.VMEM((8, LE, NY, 2, GROUP, LANES), BF),
            pltpu.VMEM((3, LE, 4, hid, LANES), BF),
            pltpu.VMEM((LE, 3, count, hid), F32),
            pltpu.VMEM((4, NZ, NC, TOK, LANES), BF),
            pltpu.VMEM((NZ, NC, 16, TOK), BF),
            pltpu.VMEM((2, NY * LE * GROUP, 4 * NC * TOK), BF),
            pltpu.VMEM((2, 4 * NC * TOK, NY * LE * GROUP), BF),
            pltpu.VMEM((2, NY * LE * GROUP, 4 * NC * TOK), BF),
            pltpu.VMEM((4, 2, NY, LE, GROUP, LANES), BF),
            pltpu.VMEM((4, 2, LE, GROUP, LANES), BF),
            dma((NZ, 2)), dma((NZ, NC)),
            dma((4, 7)), dma((4, 7)),
            dma((4, NZ)), dma((4, NZ)),
            dma((4, 2, 3, LE)), dma((4, 2, 3, LE)),
            dma((4, 2, LE)), dma((4, 2, LE)),
            dma((4, 2, NY, LE)), dma((4, 2, NY, LE)),
            dma((4,)), dma((3, LE, 4)), dma((8,)), dma((2,)),
        ],
        compiler_params=pltpu.CompilerParams(
            collective_id=0, has_side_effects=True, vmem_limit_bytes=58 << 20
        ),
        name="dispatch",
    )(mine, info, w_gate, w_up, w_down)


def return_kernel(
    rows_in, pick_in, pick_t_in, inner, w_gate, w_up, probs, info, grads, grad_probs, g_gate, g_up, g_down,
    rows, held, turned, made, x_out, x_in, kept, y_in, relay, pick, pick_t, sums, p_in, z_out, z_in, f_out, f_in, v_out, v_in, b_in, b_all, b_out,
    o_sem, w_sem, m_sem, x_send, x_recv, y_send, y_recv, r_send, r_recv, p_send, p_recv, z_send, z_recv, f_send, f_recv,
    b_send, b_recv, v_send, v_recv, g_send, g_recv, t_sem,
):
    y, z, c, x = axes()
    h = x % 2
    other = 1 - c
    sign = 1 - 2 * c
    z_long, z_short = (z + sign + NZ) % NZ, (z - sign + NZ) % NZ
    y_up, y_down = (y + 1) % NY, (y + NY - 1) % NY
    x_up, x_down = (x + 1) % NX, (x + NX - 1) % NX
    x_far = (x + 2) % NX

    barrier = pltpu.get_barrier_semaphore()
    for m in range(NZ):
        for cc in ((c, other) if m else (other,)):
            pl.semaphore_signal(barrier, inc=1, device_id={"z": (z + m) % NZ, "c": cc}, device_id_type=MESH)
    for m in range(1, NY):
        pl.semaphore_signal(barrier, inc=1, device_id={"y": (y + m) % NY}, device_id_type=MESH)
    for m in range(1, NX):
        pl.semaphore_signal(barrier, inc=1, device_id={"x": (x + m) % NX}, device_id_type=MESH)
    loads = [
        pltpu.make_async_copy(w.at[le, :, pl.ds(j * WIDE, WIDE)], held.at[i, le, j], w_sem.at[i, le, j])
        for i, w in enumerate((w_gate, w_up))
        for le in range(LE)
        for j in range(8)
    ]
    picks = [
        pltpu.make_async_copy(pick_in, pick, t_sem.at[0]),
        pltpu.make_async_copy(pick_t_in, pick_t, t_sem.at[1]),
    ]
    for copy in loads + picks:
        copy.start()
    pl.semaphore_wait(barrier, 2 * NZ - 1 + NY - 1 + NX - 1)

    waits = []

    def go(copy):
        copy.start()
        waits.append(copy)

    def x_copy(j, le):
        return remote(
            x_out.at[j, le], x_in.at[j, le], x_send.at[j, le], x_recv.at[j, le],
            x=x_up if le == 0 else x_down,
        )

    def part(j, le):
        got = jnp.dot(inner[le, 1], held[0, le, j], preferred_element_type=F32)
        got += jnp.dot(inner[le, 2], held[1, le, j], preferred_element_type=F32)
        return got.reshape(NY, 2, GROUP, WIDE)

    def fetch(slot):
        return pltpu.make_async_copy(rows_in.at[slot], rows.at[slot], o_sem.at[slot])

    def turn():
        hid = inner.shape[3]
        same = (
            lax.broadcasted_iota(jnp.int32, (hid, hid), 0) == lax.broadcasted_iota(jnp.int32, (hid, hid), 1)
        ).astype(F32).astype(BF)
        for le in range(LE):
            for i in range(3):
                turned[le, i] = nt(same, inner[le, i]).astype(BF)

    def grad_copy(i, le, q):
        out = (g_down, g_gate, g_up)[i]
        return pltpu.make_async_copy(
            made.at[i, le, q], out.at[le, :, pl.ds(q * LANES, LANES)], m_sem.at[i, le, q]
        )

    def weight_stage(le, q):
        fetch(q).wait() if le == 0 else None
        fetch(4 + q).wait() if le == 0 else None
        for i in range(3):
            some = rows[4 + q if i == 0 else q, le].reshape(NY * 2 * GROUP, LANES)
            made[i, le, q] = jnp.dot(turned[le, i], some, preferred_element_type=F32).astype(BF)
            grad_copy(i, le, q).start()

    def b_copy(m):
        return remote(
            probs.at[:, (y + NY - m) % NY], b_in.at[m], b_send.at[m], b_recv.at[m], y=(y + NY - m) % NY
        )

    for copy in loads:
        copy.wait()
    for m in range(1, NY):
        go(b_copy(m))
    for j in range(4):
        for le in range(LE):
            x_out[j, le] = part(4 * (1 - h) + j, le).astype(BF)
            go(x_copy(j, le))
    for slot in range(8):
        fetch(slot).start()
    b_own = pltpu.make_async_copy(probs.at[:, y], b_in.at[0], b_send.at[0])
    b_own.start()

    def v_copy(at, r, cc, far):
        back = PLACE[(NZ - r) % NZ]
        return remote(
            v_out.at[at, cc], v_in.at[back, c], v_send.at[at, far], v_recv.at[back, c], z=(z + r) % NZ, c=cc
        )

    for copy in picks:
        copy.wait()
    b_own.wait()
    for m in range(1, NY):
        b_copy(m).wait_recv()
    lane_row = lax.broadcasted_iota(jnp.int32, (16, 4 * NC * TOK), 0)
    for g in range(2):
        values = jnp.zeros((16, 4 * NC * TOK), F32)
        for e in range(NY * LE):
            got = jnp.dot(
                b_in[e // LE, e % LE, g][:, :GROUP],
                pick[g, pl.ds(e * GROUP, GROUP), :],
                preferred_element_type=F32,
            )
            values = jnp.where(lane_row == e, got, values)
        values = values.astype(BF)
        for i in range(8):
            v_out[4 * g + i // 2, i % 2] = values[:, i * TOK : (i + 1) * TOK]
    for r in range(NZ):
        if r:
            go(v_copy(PLACE[r], r, c, 0))
        go(v_copy(PLACE[r], r, other, 1))

    def y_copy(j, d, le):
        src = kept.at[j, le, (y + NY - d) % NY]
        sems = dict(send=y_send.at[j, d - 1, le], recv=y_recv.at[j, d - 1, le])
        if d == 1:
            return remote(src, y_in.at[j, :, 1, le], y=y_down, **sems)
        if d == 3:
            return remote(src, y_in.at[j, :, 3, le], y=y_up, **sems)
        return remote(src, relay.at[j, le], y=y_up if le == 0 else y_down, **sems)

    def relayed(j, le):
        return remote(
            relay.at[j, le], y_in.at[j, :, 2, le], r_send.at[j, le], r_recv.at[j, le],
            y=y_up if le == 0 else y_down,
        )

    def x_stage(j):
        for le in range(LE):
            own = part(4 * h + j, le)
            x_copy(j, le).wait_recv()
            kept[j, le] = (own + x_in[j, le].astype(F32)).astype(BF)
            go(y_copy(j, 2, le))
            go(y_copy(j, 1, le))
            go(y_copy(j, 3, le))
            y_in[j, :, 0, le] = kept[j, le, y]

    def relay_stage(j):
        for le in range(LE):
            y_copy(j, 2, le).wait_recv()
            go(relayed(j, le))

    def p_copy(j, g):
        return remote(
            sums.at[j, g, other], p_in.at[j, g], p_send.at[j, g], p_recv.at[j, g], c=other
        )

    def sum_stage(j):
        for le in range(LE):
            y_copy(j, 1, le).wait_recv()
            y_copy(j, 3, le).wait_recv()
            relayed(j, le).wait_recv()
        for g in (1, 0):
            got = jnp.dot(
                pick_t[g], y_in[j, g].reshape(NY * LE * GROUP, WIDE), preferred_element_type=F32
            ).astype(BF).reshape(4, NC, TOK, WIDE)
            for cc in range(NC):
                sums[j, g, cc] = got[:, cc]
            go(p_copy(j, g))

    def place(long, s):
        if s == 0:
            return 0
        if long:
            return 7 if s == 4 else 2 * s - c
        return 2 * s - 1 + c

    def z_copy(j, long, s):
        index = (s - 1) if long else (3 + s)
        return remote(
            z_out.at[j, index], z_in.at[j, index], z_send.at[j, index], z_recv.at[j, index],
            z=z_short if long else z_long,
        )

    def both(j, at):
        g, i = (0, 0) if isinstance(at, int) and at == 0 else (at // 4, at % 4)
        return sums[j, g, c, i].astype(F32) + p_in[j, g, i].astype(F32)

    def z_stage(j, s):
        if s == 4:
            for g in range(2):
                p_copy(j, g).wait_recv()
        for long in ((True, False) if s < 4 else (True,)):
            index = (s - 1) if long else (3 + s)
            total = both(j, place(long, s))
            if s < (4 if long else 3):
                z_copy(j, long, s + 1).wait_recv()
                total = total + z_in[j, index + 1].astype(F32)
            z_out[j, index] = total.astype(BF)
            go(z_copy(j, long, s))

    def f_copy(j, m):
        return remote(
            f_out.at[j], f_in.at[j, m - 1], f_send.at[j, m - 1], f_recv.at[j, m - 1], x=(x + m) % NX
        )

    def home_stage(j):
        total = both(j, 0)
        for long in (True, False):
            z_copy(j, long, 1).wait_recv()
            total = total + z_in[j, 0 if long else 4].astype(F32)
        f_out[j] = total.astype(BF)
        for m in (2, 1, 3):
            go(f_copy(j, m))

    def end_stage(j):
        for m in (1, 3, 2):
            f_copy(j, m).wait_recv()
        grads[4 * (1 - h) + j] = (f_in[j, 0].astype(F32) + f_in[j, 2].astype(F32)).astype(BF)
        grads[4 * h + j] = (f_out[j].astype(F32) + f_in[j, 1].astype(F32)).astype(BF)

    def g_copy(m):
        return remote(b_out, b_all.at[x], g_send.at[m], g_recv.at[x], x=(x + m) % NX)

    def gate_stage():
        for at in range(NZ):
            for far, cc in ((0, c), (1, other)):
                if at == 0 and far == 0:
                    continue
                remote(
                    v_out.at[at, cc], v_in.at[at, cc], v_send.at[at, far], v_recv.at[at, cc], c=other
                ).wait_recv()
        v_in[0, c] = v_out[0, c]
        row = lax.broadcasted_iota(jnp.int32, (16, TOK), 0)
        base = (y + row // LE) % NY * (NZ * NC * LE) + row % LE
        base = jnp.where(row < NY * LE, base, -NZ * NC * LE)
        found = [jnp.zeros((16, TOK), F32) for _ in range(8)]
        for r in range(NZ):
            for cc in range(NC):
                expert = (base + ((z + r) % NZ * NC + cc) * LE).astype(F32)
                value = v_in[PLACE[r], cc].astype(F32)
                for k in range(8):
                    same = info[k : k + 1].astype(F32) == expert
                    found[k] = jnp.where(same, value, found[k])
        for k in range(8):
            total = jnp.sum(found[k], axis=0, keepdims=True)
            b_out[k : k + 1] = total.astype(BF)
            b_out[8 + k : 9 + k] = total.astype(BF)
        for m in range(1, NX):
            go(g_copy(m))

    events = []
    for j in range(4):
        events += [(2 * j, j, x_stage, (j,)), (2 * j + 1, j, relay_stage, (j,)), (2 * j + 2, j, sum_stage, (j,))]
        events += [(2 * j + 3 + (4 - s), j, z_stage, (j, s)) for s in (4, 3, 2, 1)]
        events += [(2 * j + 7, j, home_stage, (j,)), (2 * j + 9, j, end_stage, (j,))]
    events.append((7.5, 0, gate_stage, ()))
    events.append((0.5, 0, turn, ()))
    for n in range(8):
        events.append((2.6 + n, 0, weight_stage, (n // 4, n % 4)))
    for _, _, stage, given in sorted(events, key=lambda e: (e[0], e[1])):
        stage(*given)
    b_all[x] = b_out[...]
    for m in range(1, NX):
        at = (x + NX - m) % NX
        remote(b_out, b_all.at[at], g_send.at[m], g_recv.at[at], x=x_up).wait_recv()
    total = (
        b_all[0].astype(F32) + b_all[1].astype(F32) + b_all[2].astype(F32) + b_all[3].astype(F32)
    )
    grad_probs[...] = total[:8] / info[...].astype(F32)[8:]
    for i in range(3):
        for le in range(LE):
            for q in range(4):
                grad_copy(i, le, q).wait()
    for copy in waits:
        copy.wait_send()


def give_back(rows, pick, pick_t, inner, w_gate, w_up, probs, info):
    hid = w_gate.shape[1]
    count = NY * 2 * GROUP
    vmem = pl.BlockSpec(memory_space=pltpu.VMEM)
    anyw = pl.BlockSpec(memory_space=pl.ANY)
    dma = pltpu.SemaphoreType.DMA
    return pl.pallas_call(
        return_kernel,
        out_shape=(
            jax.ShapeDtypeStruct((8, TOK, WIDE), BF),
            jax.ShapeDtypeStruct((8, TOK), F32),
            jax.ShapeDtypeStruct(w_gate.shape, BF),
            jax.ShapeDtypeStruct(w_gate.shape, BF),
            jax.ShapeDtypeStruct(w_gate.shape, BF),
        ),
        in_specs=[anyw, anyw, anyw, vmem, anyw, anyw, vmem, vmem],
        out_specs=(vmem, vmem, anyw, anyw, anyw),
        scratch_shapes=[
            pltpu.VMEM((8, LE, NY, 2, GROUP, LANES), BF),
            pltpu.VMEM((2, LE, 8, hid, WIDE), BF),
            pltpu.VMEM((LE, 3, hid, count), BF),
            pltpu.VMEM((3, LE, 4, hid, LANES), BF),
            pltpu.VMEM((4, LE, NY, 2, GROUP, WIDE), BF),
            pltpu.VMEM((4, LE, NY, 2, GROUP, WIDE), BF),
            pltpu.VMEM((4, LE, NY, 2, GROUP, WIDE), BF),
            pltpu.VMEM((4, 2, NY, LE, GROUP, WIDE), BF),
            pltpu.VMEM((4, LE, 2, GROUP, WIDE), BF),
            pltpu.VMEM((2, NY * LE * GROUP, 4 * NC * TOK), BF),
            pltpu.VMEM((2, 4 * NC * TOK, NY * LE * GROUP), BF),
            pltpu.VMEM((4, 2, NC, 4, TOK, WIDE), BF),
            pltpu.VMEM((4, 2, 4, TOK, WIDE), BF),
            pltpu.VMEM((4, 7, TOK, WIDE), BF),
            pltpu.VMEM((4, 7, TOK, WIDE), BF),
            pltpu.VMEM((4, TOK, WIDE), BF),
            pltpu.VMEM((4, 3, TOK, WIDE), BF),
            pltpu.VMEM((NZ, NC, 16, TOK), BF),
            pltpu.VMEM((NZ, NC, 16, TOK), BF),
            pltpu.VMEM((NY, LE, 2, 16, TOK), BF),
            pltpu.VMEM((NX, 16, TOK), BF),
            pltpu.VMEM((16, TOK), BF),
            dma((8,)), dma((2, LE, 8)), dma((3, LE, 4)),
            dma((4, LE)), dma((4, LE)),
            dma((4, 3, LE)), dma((4, 3, LE)),
            dma((4, LE)), dma((4, LE)),
            dma((4, 2)), dma((4, 2)),
            dma((4, 7)), dma((4, 7)),
            dma((4, 3)), dma((4, 3)),
            dma((NY,)), dma((NY,)),
            dma((NZ, 2)), dma((NZ, NC)),
            dma((NX,)), dma((NX,)), dma((2,)),
        ],
        compiler_params=pltpu.CompilerParams(
            collective_id=1, has_side_effects=True, vmem_limit_bytes=58 << 20
        ),
        name="give_back",
    )(rows, pick, pick_t, inner, w_gate, w_up, probs, info)


def body(tokens, grad_out, routes, probs, w_gate, w_up, w_down):
    h = lax.axis_index("x") % 2
    mine = jnp.stack(
        [
            lax.dynamic_slice_in_dim(a, h * 2 * LANES + q * LANES, LANES, axis=1)
            for a in (tokens, grad_out)
            for q in range(2)
        ]
    )
    info = jnp.concatenate([routes.T.astype(BF), probs.T], axis=0)
    rows, pick, pick_t, inner, prob = dispatch(mine, info, w_gate, w_up, w_down)
    grads, grad_probs, g_gate, g_up, g_down = give_back(
        rows, pick, pick_t, inner, w_gate, w_up, prob, info
    )
    grad_tokens = jnp.transpose(grads, (1, 0, 2)).reshape(tokens.shape)
    return (grad_tokens, grad_probs.T.astype(BF), g_gate, g_up, g_down)


def solution(mesh):
    cut = Mesh(mesh.devices.reshape(NY, NZ, NC, NX), ("y", "z", "c", "x"))
    rows = P(("y", "z", "c"), None)
    weights = P(("y", "z", "c"), "x", None)
    return jax.shard_map(
        body,
        mesh=cut,
        in_specs=(rows, rows, rows, rows, weights, weights, weights),
        out_specs=(rows, rows, weights, weights, weights),
        check_vma=False,
    )
```

```python
import jax
import jax.numpy as jnp
from jax import lax
from jax.experimental import pallas as pl
from jax.experimental.pallas import tpu as pltpu
from jax.sharding import Mesh, PartitionSpec as P

NY, NZ, NC, NX = 4, 8, 2, 4
SLOTS = 10
LE = 2
TOK = 128
GROUP = 4 * NC * SLOTS
LANES = 512
HALF = 2 * LANES
CUTS = [pl.ds(0, 384), pl.ds(384, 256), pl.ds(640, 256), pl.ds(896, 128)]
BF = jnp.bfloat16
F32 = jnp.float32
MESH = pl.DeviceIdType.MESH
PLACE = {0: 0, 1: 1, 7: 2, 2: 3, 6: 4, 3: 5, 5: 6, 4: 7}


def remote(src, dst, send, recv, **where):
    return pltpu.make_async_remote_copy(
        src_ref=src, dst_ref=dst, send_sem=send, recv_sem=recv, device_id=where, device_id_type=MESH
    )


def nt(a, b):
    return lax.dot_general(a, b, (((1,), (1,)), ((), ())), preferred_element_type=F32)


def axes():
    return tuple(lax.axis_index(n) for n in ("y", "z", "c", "x"))


def dispatch_kernel(
    mine, info, w_gate, w_up, w_down, rows_out, pick_out, pick_t_out, inner, probs,
    rows, held, acc, blocks, table, infos, pick, pick_t, pick_w, out_y, relay,
    i_send, i_recv, z_send, z_recv, p_send, p_recv, y_send, y_recv, r_send, r_recv, x_send, x_recv, l_sem, w_sem, o_sem, t_sem,
):
    y, z, c, x = axes()
    h = x % 2
    other = 1 - c
    sign = 1 - 2 * c
    z_long, z_short = (z + sign + NZ) % NZ, (z - sign + NZ) % NZ
    y_up, y_down = (y + 1) % NY, (y + NY - 1) % NY
    x_up, x_down = (x + 1) % NX, (x + NX - 1) % NX

    barrier = pltpu.get_barrier_semaphore()
    for m in range(NZ):
        for cc in ((c, other) if m else (other,)):
            pl.semaphore_signal(barrier, inc=1, device_id={"z": (z + m) % NZ, "c": cc}, device_id_type=MESH)
    for yy in (y_up, y_down):
        pl.semaphore_signal(barrier, inc=1, device_id={"y": yy}, device_id_type=MESH)
    for xx in (x_up, x_down):
        pl.semaphore_signal(barrier, inc=1, device_id={"x": xx}, device_id_type=MESH)
    loads = [
        pltpu.make_async_copy(w.at[le, :, pl.ds(q * LANES, LANES)], held.at[i, le, q], w_sem.at[i, le, q])
        for i, w in enumerate((w_gate, w_up, w_down))
        for le in range(LE)
        for q in range(4)
    ]
    for copy in loads:
        copy.start()
    row = lax.broadcasted_iota(jnp.int32, (NY * LE, TOK), 0)
    column = (y + row // LE) % NY * (NZ * NC * LE) + row % LE
    before = (
        lax.broadcasted_iota(jnp.int32, (TOK, TOK), 0) < lax.broadcasted_iota(jnp.int32, (TOK, TOK), 1)
    ).astype(F32).astype(BF)
    named = info[...].astype(F32)
    hits, weights = [], []
    for m in range(NZ):
        for cc in range(NC):
            expert = (column + ((z + m) % NZ * NC + cc) * LE).astype(F32)
            hit = jnp.zeros((NY * LE, TOK), F32)
            weight = jnp.zeros((NY * LE, TOK), F32)
            for k in range(8):
                same = named[k : k + 1] == expert
                hit = jnp.where(same, 1.0, hit)
                weight = jnp.where(same, named[8 + k : 9 + k], weight)
            hits.append(hit)
            weights.append(weight)
    ranks = jnp.dot(jnp.concatenate(hits, axis=0).astype(BF), before, preferred_element_type=F32)
    for m in range(NZ):
        for cc in range(NC):
            n = m * NC + cc
            slots = jnp.where(hits[n] > 0, ranks[n * NY * LE : (n + 1) * NY * LE], -1.0)
            table[m, cc] = jnp.concatenate([slots, weights[n]], axis=0).astype(BF)
    pick[...] = jnp.zeros_like(pick)
    pick_w[...] = jnp.zeros_like(pick_w)
    acc[...] = jnp.zeros_like(acc)
    pl.semaphore_wait(barrier, 2 * NZ - 1 + 4)

    waits = []

    def go(copy):
        copy.start()
        waits.append(copy)

    def info_copy(m, cc, far):
        at = PLACE[(NZ - m) % NZ]
        return remote(
            table.at[m, cc], infos.at[at, c], i_send.at[m, far], i_recv.at[at, c], z=(z + m) % NZ, c=cc
        )

    for m in range(NZ):
        if m:
            go(info_copy(m, c, 0))
        go(info_copy(m, other, 1))

    def place(long, s):
        if s == 0:
            return 0
        if long:
            return 7 if s == 4 else 2 * s - c
        return 2 * s - 1 + c

    def hop(k, long, s):
        index = (s - 1) if long else (3 + s)
        src = mine.at[k] if s == 1 else blocks.at[k, place(long, s - 1), c]
        return remote(
            src, blocks.at[k, place(long, s), c], z_send.at[k, index], z_recv.at[k, index],
            z=z_long if long else z_short,
        )

    def to_partner(k, at):
        src = mine.at[k] if isinstance(at, int) and at == 0 else blocks.at[k, at, c]
        return remote(src, blocks.at[k, at, c], p_send.at[k, at], p_recv.at[k, at], c=other)

    def start_chunk(k):
        go(hop(k, True, 1))
        go(hop(k, False, 1))
        go(to_partner(k, 0))
        keep = pltpu.make_async_copy(mine.at[k], blocks.at[k, 0, c], l_sem.at[k])
        keep.start()
        return keep

    keeps = {0: start_chunk(0)}

    def z_step(k, s):
        for long in ((True, False) if s < 4 else (True,)):
            hop(k, long, s).wait_recv()
            if s < (4 if long else 3):
                go(hop(k, long, s + 1))
            go(to_partner(k, place(long, s)))

    def y_piece(k, g, d, le):
        src = out_y.at[k, g, d, le]
        slot = 4 * (k // 2) + 2 * h + k % 2
        landing = rows.at[slot, le, y, g]
        sems = dict(send=y_send.at[k, g, d - 1, le], recv=y_recv.at[k, g, d - 1, le])
        if d == 1:
            return remote(src, landing, y=y_up, **sems)
        if d == 3:
            return remote(src, landing, y=y_down, **sems)
        return remote(src, relay.at[k, g, le], y=y_up if le == 0 else y_down, **sems)

    def relayed(k, g, le):
        slot = 4 * (k // 2) + 2 * h + k % 2
        came = y_down if le == 0 else y_up
        return remote(
            relay.at[k, g, le], rows.at[slot, le, came, g], r_send.at[k, g, le], r_recv.at[k, g, le],
            y=y_up if le == 0 else y_down,
        )

    def x_piece(k, g, d, le):
        slot = 4 * (k // 2) + 2 * h + k % 2
        there = rows.at[slot, le, (y + NY - d) % NY, g]
        src = out_y.at[k, g, 0, le] if d == 0 else there
        return remote(
            src, there, x_send.at[k, g, d, le], x_recv.at[k, g, d, le], x=x_up if le == 0 else x_down
        )

    def slot_of(k, half):
        return 4 * (k // 2) + 2 * half + k % 2

    def absorb(k, half):
        quarter = 2 * half + k % 2
        slot = slot_of(k, half)
        for le in range(LE):
            some = rows[slot, le].reshape(NY * 2 * GROUP, LANES)
            for i in (0, 1) if k < 2 else (2,):
                acc[le, i] += nt(some, held[i, le, quarter])
        pltpu.make_async_copy(rows.at[slot], rows_out.at[slot], o_sem.at[slot]).start()

    def x_landed(k):
        for g in range(2):
            for le in range(LE):
                for d in range(NY):
                    there = rows.at[slot_of(k, 1 - h), le, (y + NY - d) % NY, g]
                    remote(
                        there, there, x_send.at[k, g, d, le], x_recv.at[k, g, d, le],
                        x=x_up if le == 0 else x_down,
                    ).wait_recv()

    def activate():
        for le in range(LE):
            gate, up = acc[le, 0], acc[le, 1]
            sig = 1.0 / (1.0 + jnp.exp(-gate))
            act = gate * sig
            inner[le, 0] = (act * up).astype(BF)
            acc[le, 0] = up * sig * (1.0 + gate * (1.0 - sig))
            acc[le, 1] = act

    def finish():
        probs[...] = jnp.zeros_like(probs)
        ones = jnp.ones((16, acc.shape[3]), BF)
        for le in range(LE):
            back = acc[le, 2]
            inner[le, 1] = (back * acc[le, 0]).astype(BF)
            inner[le, 2] = (back * acc[le, 1]).astype(BF)
            product = (inner[le, 0].astype(F32) * back).astype(BF)
            for yy in range(NY):
                for g in range(2):
                    at = (2 * yy + g) * GROUP
                    probs[le, yy, g, :, 0:GROUP] = nt(ones, product[at : at + GROUP]).astype(BF)

    def pick_rows(k, g):
        if k in keeps:
            keeps.pop(k).wait()
        for at in range(4 * g, 4 * g + 4):
            remote(
                mine.at[k], blocks.at[k, at, other], p_send.at[k, at], p_recv.at[k, at], c=other
            ).wait_recv()
        chosen = pick[g] if k < 2 else pick_w[g]
        got = jnp.dot(
            chosen,
            blocks[k, 4 * g : 4 * g + 4].reshape(4 * NC * TOK, LANES),
            preferred_element_type=F32,
        ).astype(BF)
        out_y[k, g] = got.reshape(NY, LE, GROUP, LANES)
        for le in range(LE):
            go(y_piece(k, g, 2, le))
        for le in range(LE):
            go(y_piece(k, g, 1, le))
            go(y_piece(k, g, 3, le))
        for le in range(LE):
            go(x_piece(k, g, 0, le))
        for le in range(LE):
            rows[slot_of(k, h), le, y, g] = out_y[k, g, 0, le]

    def y_step(k, g):
        for le in range(LE):
            y_piece(k, g, 2, le).wait_recv()
            go(relayed(k, g, le))
        for le in range(LE):
            y_piece(k, g, 1, le).wait_recv()
            go(x_piece(k, g, 1, le))
            y_piece(k, g, 3, le).wait_recv()
            go(x_piece(k, g, 3, le))

    def y_last(k, g):
        for le in range(LE):
            relayed(k, g, le).wait_recv()
            go(x_piece(k, g, 2, le))

    infos[0, c] = table[0, c]

    def build(g):
        slot_row = lax.broadcasted_iota(jnp.int32, (16, TOK), 0).astype(F32)
        for at in range(4 * g, 4 * g + 4):
            if at:
                remote(info, infos.at[at, c], i_send.at[0, 0], i_recv.at[at, c], c=other).wait_recv()
            remote(info, infos.at[at, other], i_send.at[0, 0], i_recv.at[at, other], c=other).wait_recv()
            for cc in range(NC):
                i = at % 4 * NC + cc
                first, last = SLOTS * i // 16, (SLOTS * i + SLOTS - 1) // 16
                given = infos[at, cc].astype(F32)
                slots, weight = given[: NY * LE], given[NY * LE :]
                goal = jnp.where(slots >= 0, slots + float(SLOTS * i), -1.0)
                for e in range(NY * LE):
                    for tile in range(first, last + 1):
                        same = slot_row == goal[e : e + 1] - float(16 * tile)
                        put = (g, pl.ds(e * GROUP + 16 * tile, 16), pl.ds(i * TOK, TOK))
                        pick[put] = jnp.where(same, 1.0, 0.0).astype(BF)
                        pick_w[put] = jnp.where(same, weight[e : e + 1], 0.0).astype(BF)

    def pick_copies():
        return [
            pltpu.make_async_copy(pick, pick_out, t_sem.at[0]),
            pltpu.make_async_copy(pick_t, pick_t_out, t_sem.at[1]),
        ]

    def turn(g):
        same_lane = (
            lax.broadcasted_iota(jnp.int32, (TOK, TOK), 0) == lax.broadcasted_iota(jnp.int32, (TOK, TOK), 1)
        ).astype(F32).astype(BF)
        for i in range(8):
            at = pl.ds(i * TOK, TOK)
            pick_t[g, at, :] = nt(same_lane, pick[g, :, at]).astype(BF)
        if g:
            for copy in pick_copies():
                copy.start()

    def begin(k):
        keeps[k] = start_chunk(k)

    def ready():
        for copy in loads:
            copy.wait()

    def other_half(k):
        x_landed(k)
        absorb(k, 1 - h)

    events = [(5.0, build, (0,)), (9.0, build, (1,)), (16.0, ready, ()), (16.1, turn, (0,)), (21.0, turn, (1,))]
    for k in range(4):
        events += [(10 * k + 5 * n - 2, z_step, (k, n)) for n in (1, 2, 3, 4)]
        events += [(10 * k + 8.5, pick_rows, (k, 0)), (10 * k + 18.5, pick_rows, (k, 1))]
        if k:
            events.append((10 * k - 1.9, begin, (k,)))
        for g in range(2):
            n = 2 * k + g
            events += [(15 + 7.5 * n, y_step, (k, g)), (18.2 + 7.5 * n, y_last, (k, g))]
        end = 18.2 + 7.5 * (2 * k + 1)
        events += [(end + 0.1, absorb, (k, h)), (end + 6, other_half, (k,))]
    events.append((18.2 + 7.5 * 3 + 6.1, activate, ()))
    for _, stage, given in sorted(events, key=lambda e: e[0]):
        stage(*given)
    finish()
    for slot in range(8):
        pltpu.make_async_copy(rows.at[slot], rows_out.at[slot], o_sem.at[slot]).wait()
    for copy in pick_copies():
        copy.wait()
    for copy in waits:
        copy.wait_send()


def dispatch(mine, info, w_gate, w_up, w_down):
    hid = w_gate.shape[1]
    count = NY * 2 * GROUP
    vmem = pl.BlockSpec(memory_space=pltpu.VMEM)
    anyw = pl.BlockSpec(memory_space=pl.ANY)
    dma = pltpu.SemaphoreType.DMA
    return pl.pallas_call(
        dispatch_kernel,
        out_shape=(
            jax.ShapeDtypeStruct((8, LE, NY, 2, GROUP, LANES), BF),
            jax.ShapeDtypeStruct((2, NY * LE * GROUP, 4 * NC * TOK), BF),
            jax.ShapeDtypeStruct((2, 4 * NC * TOK, NY * LE * GROUP), BF),
            jax.ShapeDtypeStruct((LE, 3, count, hid), BF),
            jax.ShapeDtypeStruct((LE, NY, 2, 16, TOK), BF),
        ),
        in_specs=[vmem, vmem, anyw, anyw, anyw],
        out_specs=(anyw, anyw, anyw, vmem, vmem),
        scratch_shapes=[
            pltpu.VMEM((8, LE, NY, 2, GROUP, LANES), BF),
            pltpu.VMEM((3, LE, 4, hid, LANES), BF),
            pltpu.VMEM((LE, 3, count, hid), F32),
            pltpu.VMEM((4, NZ, NC, TOK, LANES), BF),
            pltpu.VMEM((NZ, NC, 16, TOK), BF),
            pltpu.VMEM((NZ, NC, 16, TOK), BF),
            pltpu.VMEM((2, NY * LE * GROUP, 4 * NC * TOK), BF),
            pltpu.VMEM((2, 4 * NC * TOK, NY * LE * GROUP), BF),
            pltpu.VMEM((2, NY * LE * GROUP, 4 * NC * TOK), BF),
            pltpu.VMEM((4, 2, NY, LE, GROUP, LANES), BF),
            pltpu.VMEM((4, 2, LE, GROUP, LANES), BF),
            dma((NZ, 2)), dma((NZ, NC)),
            dma((4, 7)), dma((4, 7)),
            dma((4, NZ)), dma((4, NZ)),
            dma((4, 2, 3, LE)), dma((4, 2, 3, LE)),
            dma((4, 2, LE)), dma((4, 2, LE)),
            dma((4, 2, NY, LE)), dma((4, 2, NY, LE)),
            dma((4,)), dma((3, LE, 4)), dma((8,)), dma((2,)),
        ],
        compiler_params=pltpu.CompilerParams(
            collective_id=0, has_side_effects=True, vmem_limit_bytes=58 << 20
        ),
        name="dispatch",
    )(mine, info, w_gate, w_up, w_down)


def return_kernel(
    rows_in, pick_in, pick_t_in, inner, w_gate, w_up, probs, info, grads, grad_probs, g_gate, g_up, g_down,
    rows, held, turned, made, x_out, x_in, kept, y_in, relay, pick, pick_t, sums, p_in, z_out, z_in, f_out, f_in, v_out, v_in, b_in, b_all, b_out,
    o_sem, w_sem, m_sem, x_send, x_recv, y_send, y_recv, r_send, r_recv, p_send, p_recv, z_send, z_recv, f_send, f_recv,
    b_send, b_recv, v_send, v_recv, g_send, g_recv, t_sem,
):
    y, z, c, x = axes()
    h = x % 2
    other = 1 - c
    sign = 1 - 2 * c
    z_long, z_short = (z + sign + NZ) % NZ, (z - sign + NZ) % NZ
    y_up, y_down = (y + 1) % NY, (y + NY - 1) % NY
    x_up, x_down = (x + 1) % NX, (x + NX - 1) % NX
    x_far = (x + 2) % NX

    barrier = pltpu.get_barrier_semaphore()
    for m in range(NZ):
        for cc in ((c, other) if m else (other,)):
            pl.semaphore_signal(barrier, inc=1, device_id={"z": (z + m) % NZ, "c": cc}, device_id_type=MESH)
    for m in range(1, NY):
        pl.semaphore_signal(barrier, inc=1, device_id={"y": (y + m) % NY}, device_id_type=MESH)
    for m in range(1, NX):
        pl.semaphore_signal(barrier, inc=1, device_id={"x": (x + m) % NX}, device_id_type=MESH)
    loads = [
        pltpu.make_async_copy(w.at[le, :, pl.ds(j * HALF, HALF)], held.at[i, le, j], w_sem.at[i, le, j])
        for i, w in enumerate((w_gate, w_up))
        for le in range(LE)
        for j in range(2)
    ]
    picks = [
        pltpu.make_async_copy(pick_in, pick, t_sem.at[0]),
        pltpu.make_async_copy(pick_t_in, pick_t, t_sem.at[1]),
    ]
    for copy in loads + picks:
        copy.start()
    pl.semaphore_wait(barrier, 2 * NZ - 1 + NY - 1 + NX - 1)

    waits = []

    def go(copy):
        copy.start()
        waits.append(copy)

    def x_copy(j, le):
        return remote(
            x_out.at[le, :, :, :, CUTS[j]], x_in.at[le, :, :, :, CUTS[j]], x_send.at[j, le], x_recv.at[j, le],
            x=x_up if le == 0 else x_down,
        )

    def part(half, j, le):
        got = jnp.dot(inner[le, 1], held[0, le, half, :, CUTS[j]], preferred_element_type=F32)
        got += jnp.dot(inner[le, 2], held[1, le, half, :, CUTS[j]], preferred_element_type=F32)
        return got.reshape(NY, 2, GROUP, CUTS[j].size)

    def fetch(slot):
        return pltpu.make_async_copy(rows_in.at[slot], rows.at[slot], o_sem.at[slot])

    def turn():
        hid = inner.shape[3]
        same = (
            lax.broadcasted_iota(jnp.int32, (hid, hid), 0) == lax.broadcasted_iota(jnp.int32, (hid, hid), 1)
        ).astype(F32).astype(BF)
        for le in range(LE):
            for i in range(3):
                turned[le, i] = nt(same, inner[le, i]).astype(BF)

    def grad_copy(i, le, q):
        out = (g_down, g_gate, g_up)[i]
        return pltpu.make_async_copy(
            made.at[i, le, q], out.at[le, :, pl.ds(q * LANES, LANES)], m_sem.at[i, le, q]
        )

    def weight_stage(le, q):
        fetch(q).wait() if le == 0 else None
        fetch(4 + q).wait() if le == 0 else None
        for i in range(3):
            some = rows[4 + q if i == 0 else q, le].reshape(NY * 2 * GROUP, LANES)
            made[i, le, q] = jnp.dot(turned[le, i], some, preferred_element_type=F32).astype(BF)
            grad_copy(i, le, q).start()

    def b_copy(m):
        return remote(
            probs.at[:, (y + NY - m) % NY], b_in.at[m], b_send.at[m], b_recv.at[m], y=(y + NY - m) % NY
        )

    for copy in loads:
        copy.wait()
    for m in range(1, NY):
        go(b_copy(m))
    for j in range(4):
        for le in range(LE):
            x_out[le, :, :, :, CUTS[j]] = part(1 - h, j, le).astype(BF)
            go(x_copy(j, le))
    for slot in range(8):
        fetch(slot).start()
    b_own = pltpu.make_async_copy(probs.at[:, y], b_in.at[0], b_send.at[0])
    b_own.start()

    def v_copy(at, r, cc, far):
        back = PLACE[(NZ - r) % NZ]
        return remote(
            v_out.at[at, cc], v_in.at[back, c], v_send.at[at, far], v_recv.at[back, c], z=(z + r) % NZ, c=cc
        )

    for copy in picks:
        copy.wait()
    b_own.wait()
    for m in range(1, NY):
        b_copy(m).wait_recv()
    lane_row = lax.broadcasted_iota(jnp.int32, (16, 4 * NC * TOK), 0)
    for g in range(2):
        values = jnp.zeros((16, 4 * NC * TOK), F32)
        for e in range(NY * LE):
            got = jnp.dot(
                b_in[e // LE, e % LE, g][:, :GROUP],
                pick[g, pl.ds(e * GROUP, GROUP), :],
                preferred_element_type=F32,
            )
            values = jnp.where(lane_row == e, got, values)
        values = values.astype(BF)
        for i in range(8):
            v_out[4 * g + i // 2, i % 2] = values[:, i * TOK : (i + 1) * TOK]
    for r in range(NZ):
        if r:
            go(v_copy(PLACE[r], r, c, 0))
        go(v_copy(PLACE[r], r, other, 1))

    def y_copy(j, d, le):
        src = kept.at[le, (y + NY - d) % NY, :, :, CUTS[j]]
        sems = dict(send=y_send.at[j, d - 1, le], recv=y_recv.at[j, d - 1, le])
        if d == 1:
            return remote(src, y_in.at[:, 1, le, :, CUTS[j]], y=y_down, **sems)
        if d == 3:
            return remote(src, y_in.at[:, 3, le, :, CUTS[j]], y=y_up, **sems)
        return remote(src, relay.at[le, :, :, CUTS[j]], y=y_up if le == 0 else y_down, **sems)

    def relayed(j, le):
        return remote(
            relay.at[le, :, :, CUTS[j]], y_in.at[:, 2, le, :, CUTS[j]], r_send.at[j, le], r_recv.at[j, le],
            y=y_up if le == 0 else y_down,
        )

    def x_stage(j):
        for le in range(LE):
            own = part(h, j, le)
            x_copy(j, le).wait_recv()
            kept[le, :, :, :, CUTS[j]] = (own + x_in[le, :, :, :, CUTS[j]].astype(F32)).astype(BF)
            go(y_copy(j, 2, le))
            go(y_copy(j, 1, le))
            go(y_copy(j, 3, le))
            y_in[:, 0, le, :, CUTS[j]] = kept[le, y, :, :, CUTS[j]]

    def relay_stage(j):
        for le in range(LE):
            y_copy(j, 2, le).wait_recv()
            go(relayed(j, le))

    def p_copy(j, g):
        return remote(
            sums.at[g, other, :, :, CUTS[j]], p_in.at[g, :, :, CUTS[j]], p_send.at[j, g], p_recv.at[j, g], c=other
        )

    def sum_stage(j):
        for le in range(LE):
            y_copy(j, 1, le).wait_recv()
            y_copy(j, 3, le).wait_recv()
            relayed(j, le).wait_recv()
        for g in (1, 0):
            got = jnp.dot(
                pick_t[g],
                y_in[g, :, :, :, CUTS[j]].reshape(NY * LE * GROUP, CUTS[j].size),
                preferred_element_type=F32,
            ).astype(BF).reshape(4, NC, TOK, CUTS[j].size)
            for cc in range(NC):
                sums[g, cc, :, :, CUTS[j]] = got[:, cc]
            go(p_copy(j, g))

    def place(long, s):
        if s == 0:
            return 0
        if long:
            return 7 if s == 4 else 2 * s - c
        return 2 * s - 1 + c

    def z_copy(j, long, s):
        index = (s - 1) if long else (3 + s)
        return remote(
            z_out.at[index, :, CUTS[j]], z_in.at[index, :, CUTS[j]], z_send.at[j, index], z_recv.at[j, index],
            z=z_short if long else z_long,
        )

    def both(j, at):
        g, i = (0, 0) if isinstance(at, int) and at == 0 else (at // 4, at % 4)
        return sums[g, c, i, :, CUTS[j]].astype(F32) + p_in[g, i, :, CUTS[j]].astype(F32)

    def z_stage(j, s):
        if s == 4:
            for g in range(2):
                p_copy(j, g).wait_recv()
        for long in ((True, False) if s < 4 else (True,)):
            index = (s - 1) if long else (3 + s)
            total = both(j, place(long, s))
            if s < (4 if long else 3):
                z_copy(j, long, s + 1).wait_recv()
                total = total + z_in[index + 1, :, CUTS[j]].astype(F32)
            z_out[index, :, CUTS[j]] = total.astype(BF)
            go(z_copy(j, long, s))

    def f_copy(j, m):
        return remote(
            f_out.at[:, CUTS[j]], f_in.at[m - 1, :, CUTS[j]], f_send.at[j, m - 1], f_recv.at[j, m - 1], x=(x + m) % NX
        )

    def home_stage(j):
        total = both(j, 0)
        for long in (True, False):
            z_copy(j, long, 1).wait_recv()
            total = total + z_in[0 if long else 4, :, CUTS[j]].astype(F32)
        f_out[:, CUTS[j]] = total.astype(BF)
        for m in (2, 1, 3):
            go(f_copy(j, m))

    def end_stage(j):
        for m in (1, 3, 2):
            f_copy(j, m).wait_recv()
        cut = CUTS[j]
        grads[1 - h, :, cut] = (f_in[0, :, cut].astype(F32) + f_in[2, :, cut].astype(F32)).astype(BF)
        grads[h, :, cut] = (f_out[:, cut].astype(F32) + f_in[1, :, cut].astype(F32)).astype(BF)

    def g_copy(m):
        return remote(b_out, b_all.at[x], g_send.at[m], g_recv.at[x], x=(x + m) % NX)

    def gate_stage():
        for at in range(NZ):
            for far, cc in ((0, c), (1, other)):
                if at == 0 and far == 0:
                    continue
                remote(
                    v_out.at[at, cc], v_in.at[at, cc], v_send.at[at, far], v_recv.at[at, cc], c=other
                ).wait_recv()
        v_in[0, c] = v_out[0, c]
        row = lax.broadcasted_iota(jnp.int32, (16, TOK), 0)
        base = (y + row // LE) % NY * (NZ * NC * LE) + row % LE
        base = jnp.where(row < NY * LE, base, -NZ * NC * LE)
        found = [jnp.zeros((16, TOK), F32) for _ in range(8)]
        for r in range(NZ):
            for cc in range(NC):
                expert = (base + ((z + r) % NZ * NC + cc) * LE).astype(F32)
                value = v_in[PLACE[r], cc].astype(F32)
                for k in range(8):
                    same = info[k : k + 1].astype(F32) == expert
                    found[k] = jnp.where(same, value, found[k])
        for k in range(8):
            total = jnp.sum(found[k], axis=0, keepdims=True)
            b_out[k : k + 1] = total.astype(BF)
            b_out[8 + k : 9 + k] = total.astype(BF)
        for m in range(1, NX):
            go(g_copy(m))

    events = [(9.0, 0, turn, ()), (33.0, 0, gate_stage, ())]
    events += [(10.0 + 2 * n, 0, weight_stage, (n // 4, n % 4)) for n in range(8)]
    for j, cut in enumerate(CUTS):
        wide = cut.size / 256
        at = 8 + 32 * (cut.start + cut.size) / HALF
        events += [(at, j, x_stage, (j,)), (at + 1.5 + 2 * wide, j, relay_stage, (j,))]
        at += 3 + 7 * wide
        events.append((at, j, sum_stage, (j,)))
        at += 1 + 1.5 * wide
        for n in (4, 3, 2, 1):
            events.append((at, j, z_stage, (j, n)))
            at += 1.5 + 1.6 * wide
        events += [(at, j, home_stage, (j,)), (at + 2 + 3 * wide, j, end_stage, (j,))]
    for _, _, stage, given in sorted(events, key=lambda e: (e[0], e[1])):
        stage(*given)
    b_all[x] = b_out[...]
    for m in range(1, NX):
        at = (x + NX - m) % NX
        remote(b_out, b_all.at[at], g_send.at[m], g_recv.at[at], x=x_up).wait_recv()
    total = (
        b_all[0].astype(F32) + b_all[1].astype(F32) + b_all[2].astype(F32) + b_all[3].astype(F32)
    )
    grad_probs[...] = total[:8] / info[...].astype(F32)[8:]
    for i in range(3):
        for le in range(LE):
            for q in range(4):
                grad_copy(i, le, q).wait()
    for copy in waits:
        copy.wait_send()


def give_back(rows, pick, pick_t, inner, w_gate, w_up, probs, info):
    hid = w_gate.shape[1]
    count = NY * 2 * GROUP
    vmem = pl.BlockSpec(memory_space=pltpu.VMEM)
    anyw = pl.BlockSpec(memory_space=pl.ANY)
    dma = pltpu.SemaphoreType.DMA
    return pl.pallas_call(
        return_kernel,
        out_shape=(
            jax.ShapeDtypeStruct((2, TOK, HALF), BF),
            jax.ShapeDtypeStruct((8, TOK), F32),
            jax.ShapeDtypeStruct(w_gate.shape, BF),
            jax.ShapeDtypeStruct(w_gate.shape, BF),
            jax.ShapeDtypeStruct(w_gate.shape, BF),
        ),
        in_specs=[anyw, anyw, anyw, vmem, anyw, anyw, vmem, vmem],
        out_specs=(vmem, vmem, anyw, anyw, anyw),
        scratch_shapes=[
            pltpu.VMEM((8, LE, NY, 2, GROUP, LANES), BF),
            pltpu.VMEM((2, LE, 2, hid, HALF), BF),
            pltpu.VMEM((LE, 3, hid, count), BF),
            pltpu.VMEM((3, LE, 4, hid, LANES), BF),
            pltpu.VMEM((LE, NY, 2, GROUP, HALF), BF),
            pltpu.VMEM((LE, NY, 2, GROUP, HALF), BF),
            pltpu.VMEM((LE, NY, 2, GROUP, HALF), BF),
            pltpu.VMEM((2, NY, LE, GROUP, HALF), BF),
            pltpu.VMEM((LE, 2, GROUP, HALF), BF),
            pltpu.VMEM((2, NY * LE * GROUP, 4 * NC * TOK), BF),
            pltpu.VMEM((2, 4 * NC * TOK, NY * LE * GROUP), BF),
            pltpu.VMEM((2, NC, 4, TOK, HALF), BF),
            pltpu.VMEM((2, 4, TOK, HALF), BF),
            pltpu.VMEM((7, TOK, HALF), BF),
            pltpu.VMEM((7, TOK, HALF), BF),
            pltpu.VMEM((TOK, HALF), BF),
            pltpu.VMEM((3, TOK, HALF), BF),
            pltpu.VMEM((NZ, NC, 16, TOK), BF),
            pltpu.VMEM((NZ, NC, 16, TOK), BF),
            pltpu.VMEM((NY, LE, 2, 16, TOK), BF),
            pltpu.VMEM((NX, 16, TOK), BF),
            pltpu.VMEM((16, TOK), BF),
            dma((8,)), dma((2, LE, 2)), dma((3, LE, 4)),
            dma((4, LE)), dma((4, LE)),
            dma((4, 3, LE)), dma((4, 3, LE)),
            dma((4, LE)), dma((4, LE)),
            dma((4, 2)), dma((4, 2)),
            dma((4, 7)), dma((4, 7)),
            dma((4, 3)), dma((4, 3)),
            dma((NY,)), dma((NY,)),
            dma((NZ, 2)), dma((NZ, NC)),
            dma((NX,)), dma((NX,)), dma((2,)),
        ],
        compiler_params=pltpu.CompilerParams(
            collective_id=1, has_side_effects=True, vmem_limit_bytes=58 << 20
        ),
        name="give_back",
    )(rows, pick, pick_t, inner, w_gate, w_up, probs, info)


def body(tokens, grad_out, routes, probs, w_gate, w_up, w_down):
    h = lax.axis_index("x") % 2
    mine = jnp.stack(
        [
            lax.dynamic_slice_in_dim(a, h * 2 * LANES + q * LANES, LANES, axis=1)
            for a in (tokens, grad_out)
            for q in range(2)
        ]
    )
    info = jnp.concatenate([routes.T.astype(BF), probs.T], axis=0)
    rows, pick, pick_t, inner, prob = dispatch(mine, info, w_gate, w_up, w_down)
    grads, grad_probs, g_gate, g_up, g_down = give_back(
        rows, pick, pick_t, inner, w_gate, w_up, prob, info
    )
    grad_tokens = jnp.transpose(grads, (1, 0, 2)).reshape(tokens.shape)
    return (grad_tokens, grad_probs.T.astype(BF), g_gate, g_up, g_down)


def solution(mesh):
    cut = Mesh(mesh.devices.reshape(NY, NZ, NC, NX), ("y", "z", "c", "x"))
    rows = P(("y", "z", "c"), None)
    weights = P(("y", "z", "c"), "x", None)
    return jax.shard_map(
        body,
        mesh=cut,
        in_specs=(rows, rows, rows, rows, weights, weights, weights),
        out_specs=(rows, rows, weights, weights, weights),
        check_vma=False,
    )
```

```python
import jax
import jax.numpy as jnp
from jax import lax
from jax.experimental import pallas as pl
from jax.experimental.pallas import tpu as pltpu
from jax.sharding import Mesh, PartitionSpec as P

NY, NZ, NC, NX = 4, 8, 2, 4
SLOTS = 10
LE = 2
TOK = 128
GROUP = 4 * NC * SLOTS
LANES = 512
HALF = 2 * LANES
CUTS = [pl.ds(0, 384), pl.ds(384, 256), pl.ds(640, 256), pl.ds(896, 128)]
BF = jnp.bfloat16
F32 = jnp.float32
MESH = pl.DeviceIdType.MESH
PLACE = {0: 0, 1: 1, 7: 2, 2: 3, 6: 4, 3: 5, 5: 6, 4: 7}


def remote(src, dst, send, recv, **where):
    return pltpu.make_async_remote_copy(
        src_ref=src, dst_ref=dst, send_sem=send, recv_sem=recv, device_id=where, device_id_type=MESH
    )


def nt(a, b):
    return lax.dot_general(a, b, (((1,), (1,)), ((), ())), preferred_element_type=F32)


def axes():
    return tuple(lax.axis_index(n) for n in ("y", "z", "c", "x"))


def dispatch_kernel(
    tokens, grad_out, info, w_gate, w_up, w_down, rows_out, pick_out, pick_t_out, inner, probs,
    rows, held, acc, blocks, table, infos, pick, pick_t, pick_w, out_y, relay,
    i_send, i_recv, z_send, z_recv, p_send, p_recv, y_send, y_recv, r_send, r_recv, x_send, x_recv, l_sem, w_sem, o_sem, t_sem,
):
    y, z, c, x = axes()
    h = x % 2
    other = 1 - c
    sign = 1 - 2 * c
    z_long, z_short = (z + sign + NZ) % NZ, (z - sign + NZ) % NZ
    y_up, y_down = (y + 1) % NY, (y + NY - 1) % NY
    x_up, x_down = (x + 1) % NX, (x + NX - 1) % NX

    barrier = pltpu.get_barrier_semaphore()
    for m in range(NZ):
        for cc in ((c, other) if m else (other,)):
            pl.semaphore_signal(barrier, inc=1, device_id={"z": (z + m) % NZ, "c": cc}, device_id_type=MESH)
    for yy in (y_up, y_down):
        pl.semaphore_signal(barrier, inc=1, device_id={"y": yy}, device_id_type=MESH)
    for xx in (x_up, x_down):
        pl.semaphore_signal(barrier, inc=1, device_id={"x": xx}, device_id_type=MESH)
    loads = [
        pltpu.make_async_copy(w.at[le, :, pl.ds(q * LANES, LANES)], held.at[i, le, q], w_sem.at[i, le, q])
        for i, w in enumerate((w_gate, w_up, w_down))
        for le in range(LE)
        for q in range(4)
    ]
    for copy in loads:
        copy.start()
    row = lax.broadcasted_iota(jnp.int32, (NY * LE, TOK), 0)
    column = (y + row // LE) % NY * (NZ * NC * LE) + row % LE
    before = (
        lax.broadcasted_iota(jnp.int32, (TOK, TOK), 0) < lax.broadcasted_iota(jnp.int32, (TOK, TOK), 1)
    ).astype(F32).astype(BF)
    named = info[...].astype(F32)
    hits, weights = [], []
    for m in range(NZ):
        for cc in range(NC):
            expert = (column + ((z + m) % NZ * NC + cc) * LE).astype(F32)
            hit = jnp.zeros((NY * LE, TOK), F32)
            weight = jnp.zeros((NY * LE, TOK), F32)
            for k in range(8):
                same = named[k : k + 1] == expert
                hit = jnp.where(same, 1.0, hit)
                weight = jnp.where(same, named[8 + k : 9 + k], weight)
            hits.append(hit)
            weights.append(weight)
    ranks = jnp.dot(jnp.concatenate(hits, axis=0).astype(BF), before, preferred_element_type=F32)
    for m in range(NZ):
        for cc in range(NC):
            n = m * NC + cc
            slots = jnp.where(hits[n] > 0, ranks[n * NY * LE : (n + 1) * NY * LE], -1.0)
            table[m, cc] = jnp.concatenate([slots, weights[n]], axis=0).astype(BF)
    pick[...] = jnp.zeros_like(pick)
    pick_w[...] = jnp.zeros_like(pick_w)
    acc[...] = jnp.zeros_like(acc)
    pl.semaphore_wait(barrier, 2 * NZ - 1 + 4)

    waits = []

    def go(copy):
        copy.start()
        waits.append(copy)

    def info_copy(m, cc, far):
        at = PLACE[(NZ - m) % NZ]
        return remote(
            table.at[m, cc], infos.at[at, c], i_send.at[m, far], i_recv.at[at, c], z=(z + m) % NZ, c=cc
        )

    for m in range(NZ):
        if m:
            go(info_copy(m, c, 0))
        go(info_copy(m, other, 1))

    def place(long, s):
        if s == 0:
            return 0
        if long:
            return 7 if s == 4 else 2 * s - c
        return 2 * s - 1 + c

    def hop(k, long, s):
        index = (s - 1) if long else (3 + s)
        src = mine(k) if s == 1 else blocks.at[k, place(long, s - 1), c]
        return remote(
            src, blocks.at[k, place(long, s), c], z_send.at[k, index], z_recv.at[k, index],
            z=z_long if long else z_short,
        )

    def to_partner(k, at):
        src = mine(k) if isinstance(at, int) and at == 0 else blocks.at[k, at, c]
        return remote(src, blocks.at[k, at, c], p_send.at[k, at], p_recv.at[k, at], c=other)

    def mine(k):
        at = pl.multiple_of(h * HALF + k % 2 * LANES, LANES)
        return (tokens if k < 2 else grad_out).at[:, pl.ds(at, LANES)]

    def start_chunk(k):
        go(hop(k, True, 1))
        go(hop(k, False, 1))
        go(to_partner(k, 0))
        keep = pltpu.make_async_copy(mine(k), blocks.at[k, 0, c], l_sem.at[k])
        keep.start()
        return keep

    keeps = {0: start_chunk(0)}

    def z_step(k, s):
        for long in ((True, False) if s < 4 else (True,)):
            hop(k, long, s).wait_recv()
            if s < (4 if long else 3):
                go(hop(k, long, s + 1))
            go(to_partner(k, place(long, s)))

    def y_piece(k, g, d, le):
        src = out_y.at[k, g, d, le]
        slot = 4 * (k // 2) + 2 * h + k % 2
        landing = rows.at[slot, le, y, g]
        sems = dict(send=y_send.at[k, g, d - 1, le], recv=y_recv.at[k, g, d - 1, le])
        if d == 1:
            return remote(src, landing, y=y_up, **sems)
        if d == 3:
            return remote(src, landing, y=y_down, **sems)
        return remote(src, relay.at[k, g, le], y=y_up if le == 0 else y_down, **sems)

    def relayed(k, g, le):
        slot = 4 * (k // 2) + 2 * h + k % 2
        came = y_down if le == 0 else y_up
        return remote(
            relay.at[k, g, le], rows.at[slot, le, came, g], r_send.at[k, g, le], r_recv.at[k, g, le],
            y=y_up if le == 0 else y_down,
        )

    def x_piece(k, g, d, le):
        slot = 4 * (k // 2) + 2 * h + k % 2
        there = rows.at[slot, le, (y + NY - d) % NY, g]
        src = out_y.at[k, g, 0, le] if d == 0 else there
        return remote(
            src, there, x_send.at[k, g, d, le], x_recv.at[k, g, d, le], x=x_up if le == 0 else x_down
        )

    def slot_of(k, half):
        return 4 * (k // 2) + 2 * half + k % 2

    def absorb(k, half):
        quarter = 2 * half + k % 2
        slot = slot_of(k, half)
        for le in range(LE):
            some = rows[slot, le].reshape(NY * 2 * GROUP, LANES)
            for i in (0, 1) if k < 2 else (2,):
                acc[le, i] += nt(some, held[i, le, quarter])
        pltpu.make_async_copy(rows.at[slot], rows_out.at[slot], o_sem.at[slot]).start()

    def x_landed(k):
        for g in range(2):
            for le in range(LE):
                for d in range(NY):
                    there = rows.at[slot_of(k, 1 - h), le, (y + NY - d) % NY, g]
                    remote(
                        there, there, x_send.at[k, g, d, le], x_recv.at[k, g, d, le],
                        x=x_up if le == 0 else x_down,
                    ).wait_recv()

    def activate():
        for le in range(LE):
            gate, up = acc[le, 0], acc[le, 1]
            sig = 1.0 / (1.0 + jnp.exp(-gate))
            act = gate * sig
            inner[le, 0] = (act * up).astype(BF)
            acc[le, 0] = up * sig * (1.0 + gate * (1.0 - sig))
            acc[le, 1] = act

    def finish():
        probs[...] = jnp.zeros_like(probs)
        ones = jnp.ones((16, acc.shape[3]), BF)
        for le in range(LE):
            back = acc[le, 2]
            inner[le, 1] = (back * acc[le, 0]).astype(BF)
            inner[le, 2] = (back * acc[le, 1]).astype(BF)
            product = (inner[le, 0].astype(F32) * back).astype(BF)
            for yy in range(NY):
                for g in range(2):
                    at = (2 * yy + g) * GROUP
                    probs[le, yy, g, :, 0:GROUP] = nt(ones, product[at : at + GROUP]).astype(BF)

    def pick_rows(k, g):
        if k in keeps:
            keeps.pop(k).wait()
        for at in range(4 * g, 4 * g + 4):
            remote(
                mine(k), blocks.at[k, at, other], p_send.at[k, at], p_recv.at[k, at], c=other
            ).wait_recv()
        chosen = pick[g] if k < 2 else pick_w[g]
        got = jnp.dot(
            chosen,
            blocks[k, 4 * g : 4 * g + 4].reshape(4 * NC * TOK, LANES),
            preferred_element_type=F32,
        ).astype(BF)
        out_y[k, g] = got.reshape(NY, LE, GROUP, LANES)
        for le in range(LE):
            go(y_piece(k, g, 2, le))
        for le in range(LE):
            go(y_piece(k, g, 1, le))
            go(y_piece(k, g, 3, le))
        for le in range(LE):
            go(x_piece(k, g, 0, le))
        for le in range(LE):
            rows[slot_of(k, h), le, y, g] = out_y[k, g, 0, le]

    def y_step(k, g):
        for le in range(LE):
            y_piece(k, g, 2, le).wait_recv()
            go(relayed(k, g, le))
        for le in range(LE):
            y_piece(k, g, 1, le).wait_recv()
            go(x_piece(k, g, 1, le))
            y_piece(k, g, 3, le).wait_recv()
            go(x_piece(k, g, 3, le))

    def y_last(k, g):
        for le in range(LE):
            relayed(k, g, le).wait_recv()
            go(x_piece(k, g, 2, le))

    infos[0, c] = table[0, c]

    def build(g):
        slot_row = lax.broadcasted_iota(jnp.int32, (16, TOK), 0).astype(F32)
        for at in range(4 * g, 4 * g + 4):
            if at:
                remote(info, infos.at[at, c], i_send.at[0, 0], i_recv.at[at, c], c=other).wait_recv()
            remote(info, infos.at[at, other], i_send.at[0, 0], i_recv.at[at, other], c=other).wait_recv()
            for cc in range(NC):
                i = at % 4 * NC + cc
                first, last = SLOTS * i // 16, (SLOTS * i + SLOTS - 1) // 16
                given = infos[at, cc].astype(F32)
                slots, weight = given[: NY * LE], given[NY * LE :]
                goal = jnp.where(slots >= 0, slots + float(SLOTS * i), -1.0)
                for e in range(NY * LE):
                    for tile in range(first, last + 1):
                        same = slot_row == goal[e : e + 1] - float(16 * tile)
                        put = (g, pl.ds(e * GROUP + 16 * tile, 16), pl.ds(i * TOK, TOK))
                        pick[put] = jnp.where(same, 1.0, 0.0).astype(BF)
                        pick_w[put] = jnp.where(same, weight[e : e + 1], 0.0).astype(BF)

    def pick_copies():
        return [
            pltpu.make_async_copy(pick, pick_out, t_sem.at[0]),
            pltpu.make_async_copy(pick_t, pick_t_out, t_sem.at[1]),
        ]

    def turn(g):
        same_lane = (
            lax.broadcasted_iota(jnp.int32, (TOK, TOK), 0) == lax.broadcasted_iota(jnp.int32, (TOK, TOK), 1)
        ).astype(F32).astype(BF)
        for i in range(8):
            at = pl.ds(i * TOK, TOK)
            pick_t[g, at, :] = nt(same_lane, pick[g, :, at]).astype(BF)
        if g:
            for copy in pick_copies():
                copy.start()

    def begin(k):
        keeps[k] = start_chunk(k)

    def ready():
        for copy in loads:
            copy.wait()

    def other_half(k):
        x_landed(k)
        absorb(k, 1 - h)

    events = [(4.2, build, (0,)), (8.6, build, (1,)), (16.0, ready, ()), (16.1, turn, (0,)), (18.0, turn, (1,))]
    for k in range(4):
        start = 16 * k
        events += [(start + 4 * n, z_step, (k, n)) for n in (1, 2, 3, 4)]
        events += [(start + 8.5, pick_rows, (k, 0)), (start + 16.7, pick_rows, (k, 1))]
        if k:
            events.append((start - 7.95, begin, (k,)))
        for g in range(2):
            at = start + 20.5 + 8 * g
            events += [(at, y_step, (k, g)), (at + 7.9, y_last, (k, g))]
        events += [(start + 36.5, absorb, (k, h)), (start + 42.4, other_half, (k,))]
    events.append((58.5, activate, ()))
    for _, stage, given in sorted(events, key=lambda e: e[0]):
        stage(*given)
    finish()
    for slot in range(8):
        pltpu.make_async_copy(rows.at[slot], rows_out.at[slot], o_sem.at[slot]).wait()
    for copy in pick_copies():
        copy.wait()
    for copy in waits:
        copy.wait_send()


def dispatch(tokens, grad_out, info, w_gate, w_up, w_down):
    hid = w_gate.shape[1]
    count = NY * 2 * GROUP
    vmem = pl.BlockSpec(memory_space=pltpu.VMEM)
    anyw = pl.BlockSpec(memory_space=pl.ANY)
    dma = pltpu.SemaphoreType.DMA
    return pl.pallas_call(
        dispatch_kernel,
        out_shape=(
            jax.ShapeDtypeStruct((8, LE, NY, 2, GROUP, LANES), BF),
            jax.ShapeDtypeStruct((2, NY * LE * GROUP, 4 * NC * TOK), BF),
            jax.ShapeDtypeStruct((2, 4 * NC * TOK, NY * LE * GROUP), BF),
            jax.ShapeDtypeStruct((LE, 3, count, hid), BF),
            jax.ShapeDtypeStruct((LE, NY, 2, 16, TOK), BF),
        ),
        in_specs=[anyw, anyw, vmem, anyw, anyw, anyw],
        out_specs=(anyw, anyw, anyw, vmem, vmem),
        scratch_shapes=[
            pltpu.VMEM((8, LE, NY, 2, GROUP, LANES), BF),
            pltpu.VMEM((3, LE, 4, hid, LANES), BF),
            pltpu.VMEM((LE, 3, count, hid), F32),
            pltpu.VMEM((4, NZ, NC, TOK, LANES), BF),
            pltpu.VMEM((NZ, NC, 16, TOK), BF),
            pltpu.VMEM((NZ, NC, 16, TOK), BF),
            pltpu.VMEM((2, NY * LE * GROUP, 4 * NC * TOK), BF),
            pltpu.VMEM((2, 4 * NC * TOK, NY * LE * GROUP), BF),
            pltpu.VMEM((2, NY * LE * GROUP, 4 * NC * TOK), BF),
            pltpu.VMEM((4, 2, NY, LE, GROUP, LANES), BF),
            pltpu.VMEM((4, 2, LE, GROUP, LANES), BF),
            dma((NZ, 2)), dma((NZ, NC)),
            dma((4, 7)), dma((4, 7)),
            dma((4, NZ)), dma((4, NZ)),
            dma((4, 2, 3, LE)), dma((4, 2, 3, LE)),
            dma((4, 2, LE)), dma((4, 2, LE)),
            dma((4, 2, NY, LE)), dma((4, 2, NY, LE)),
            dma((4,)), dma((3, LE, 4)), dma((8,)), dma((2,)),
        ],
        compiler_params=pltpu.CompilerParams(
            collective_id=0, has_side_effects=True, vmem_limit_bytes=58 << 20
        ),
        name="dispatch",
    )(tokens, grad_out, info, w_gate, w_up, w_down)


def return_kernel(
    rows_in, pick_in, pick_t_in, inner, w_gate, w_up, probs, info, grads, grad_probs, g_gate, g_up, g_down,
    rows, held, turned, made, x_out, x_in, kept, y_in, relay, pick, pick_t, sums, p_in, z_out, z_in, f_out, f_in, v_out, v_in, b_in, b_all, b_out,
    o_sem, w_sem, m_sem, x_send, x_recv, y_send, y_recv, r_send, r_recv, p_send, p_recv, z_send, z_recv, f_send, f_recv,
    b_send, b_recv, v_send, v_recv, g_send, g_recv, t_sem,
):
    y, z, c, x = axes()
    h = x % 2
    other = 1 - c
    sign = 1 - 2 * c
    z_long, z_short = (z + sign + NZ) % NZ, (z - sign + NZ) % NZ
    y_up, y_down = (y + 1) % NY, (y + NY - 1) % NY
    x_up, x_down = (x + 1) % NX, (x + NX - 1) % NX
    x_far = (x + 2) % NX

    barrier = pltpu.get_barrier_semaphore()
    for m in range(NZ):
        for cc in ((c, other) if m else (other,)):
            pl.semaphore_signal(barrier, inc=1, device_id={"z": (z + m) % NZ, "c": cc}, device_id_type=MESH)
    for m in range(1, NY):
        pl.semaphore_signal(barrier, inc=1, device_id={"y": (y + m) % NY}, device_id_type=MESH)
    for m in range(1, NX):
        pl.semaphore_signal(barrier, inc=1, device_id={"x": (x + m) % NX}, device_id_type=MESH)
    loads = [
        pltpu.make_async_copy(w.at[le, :, pl.ds(j * HALF, HALF)], held.at[i, le, j], w_sem.at[i, le, j])
        for i, w in enumerate((w_gate, w_up))
        for le in range(LE)
        for j in range(2)
    ]
    picks = [
        pltpu.make_async_copy(pick_in, pick, t_sem.at[0]),
        pltpu.make_async_copy(pick_t_in, pick_t, t_sem.at[1]),
    ]
    for copy in loads + picks:
        copy.start()
    pl.semaphore_wait(barrier, 2 * NZ - 1 + NY - 1 + NX - 1)

    waits = []

    def go(copy):
        copy.start()
        waits.append(copy)

    def x_copy(j, le):
        return remote(
            x_out.at[le, :, :, :, CUTS[j]], x_in.at[le, :, :, :, CUTS[j]], x_send.at[j, le], x_recv.at[j, le],
            x=x_up if le == 0 else x_down,
        )

    def part(half, j, le):
        got = jnp.dot(inner[le, 1], held[0, le, half, :, CUTS[j]], preferred_element_type=F32)
        got += jnp.dot(inner[le, 2], held[1, le, half, :, CUTS[j]], preferred_element_type=F32)
        return got.reshape(NY, 2, GROUP, CUTS[j].size)

    def fetch(slot):
        return pltpu.make_async_copy(rows_in.at[slot], rows.at[slot], o_sem.at[slot])

    def turn():
        hid = inner.shape[3]
        same = (
            lax.broadcasted_iota(jnp.int32, (hid, hid), 0) == lax.broadcasted_iota(jnp.int32, (hid, hid), 1)
        ).astype(F32).astype(BF)
        for le in range(LE):
            for i in range(3):
                turned[le, i] = nt(same, inner[le, i]).astype(BF)

    def grad_copy(i, le, q):
        out = (g_down, g_gate, g_up)[i]
        return pltpu.make_async_copy(
            made.at[i, le, q], out.at[le, :, pl.ds(q * LANES, LANES)], m_sem.at[i, le, q]
        )

    def weight_stage(le, q):
        fetch(q).wait() if le == 0 else None
        fetch(4 + q).wait() if le == 0 else None
        for i in range(3):
            some = rows[4 + q if i == 0 else q, le].reshape(NY * 2 * GROUP, LANES)
            made[i, le, q] = jnp.dot(turned[le, i], some, preferred_element_type=F32).astype(BF)
            grad_copy(i, le, q).start()

    def b_copy(m):
        return remote(
            probs.at[:, (y + NY - m) % NY], b_in.at[m], b_send.at[m], b_recv.at[m], y=(y + NY - m) % NY
        )

    for copy in loads:
        copy.wait()
    for m in range(1, NY):
        go(b_copy(m))
    for j in range(4):
        for le in range(LE):
            x_out[le, :, :, :, CUTS[j]] = part(1 - h, j, le).astype(BF)
            go(x_copy(j, le))
    for slot in range(8):
        fetch(slot).start()
    b_own = pltpu.make_async_copy(probs.at[:, y], b_in.at[0], b_send.at[0])
    b_own.start()

    def v_copy(at, r, cc, far):
        back = PLACE[(NZ - r) % NZ]
        return remote(
            v_out.at[at, cc], v_in.at[back, c], v_send.at[at, far], v_recv.at[back, c], z=(z + r) % NZ, c=cc
        )

    for copy in picks:
        copy.wait()
    b_own.wait()
    for m in range(1, NY):
        b_copy(m).wait_recv()
    lane_row = lax.broadcasted_iota(jnp.int32, (16, 4 * NC * TOK), 0)
    for g in range(2):
        values = jnp.zeros((16, 4 * NC * TOK), F32)
        for e in range(NY * LE):
            got = jnp.dot(
                b_in[e // LE, e % LE, g][:, :GROUP],
                pick[g, pl.ds(e * GROUP, GROUP), :],
                preferred_element_type=F32,
            )
            values = jnp.where(lane_row == e, got, values)
        values = values.astype(BF)
        for i in range(8):
            v_out[4 * g + i // 2, i % 2] = values[:, i * TOK : (i + 1) * TOK]
    for r in range(NZ):
        if r:
            go(v_copy(PLACE[r], r, c, 0))
        go(v_copy(PLACE[r], r, other, 1))

    def y_copy(j, d, le):
        src = kept.at[le, (y + NY - d) % NY, :, :, CUTS[j]]
        sems = dict(send=y_send.at[j, d - 1, le], recv=y_recv.at[j, d - 1, le])
        if d == 1:
            return remote(src, y_in.at[:, 1, le, :, CUTS[j]], y=y_down, **sems)
        if d == 3:
            return remote(src, y_in.at[:, 3, le, :, CUTS[j]], y=y_up, **sems)
        return remote(src, relay.at[le, :, :, CUTS[j]], y=y_up if le == 0 else y_down, **sems)

    def relayed(j, le):
        return remote(
            relay.at[le, :, :, CUTS[j]], y_in.at[:, 2, le, :, CUTS[j]], r_send.at[j, le], r_recv.at[j, le],
            y=y_up if le == 0 else y_down,
        )

    def x_stage(j):
        for le in range(LE):
            own = part(h, j, le)
            x_copy(j, le).wait_recv()
            kept[le, :, :, :, CUTS[j]] = (own + x_in[le, :, :, :, CUTS[j]].astype(F32)).astype(BF)
            go(y_copy(j, 2, le))
            go(y_copy(j, 1, le))
            go(y_copy(j, 3, le))
            y_in[:, 0, le, :, CUTS[j]] = kept[le, y, :, :, CUTS[j]]

    def relay_stage(j):
        for le in range(LE):
            y_copy(j, 2, le).wait_recv()
            go(relayed(j, le))

    def p_copy(j, g):
        return remote(
            sums.at[g, other, :, :, CUTS[j]], p_in.at[g, :, :, CUTS[j]], p_send.at[j, g], p_recv.at[j, g], c=other
        )

    def sum_stage(j):
        for le in range(LE):
            y_copy(j, 1, le).wait_recv()
            y_copy(j, 3, le).wait_recv()
            relayed(j, le).wait_recv()
        for g in (1, 0):
            got = jnp.dot(
                pick_t[g],
                y_in[g, :, :, :, CUTS[j]].reshape(NY * LE * GROUP, CUTS[j].size),
                preferred_element_type=F32,
            ).astype(BF).reshape(4, NC, TOK, CUTS[j].size)
            for cc in range(NC):
                sums[g, cc, :, :, CUTS[j]] = got[:, cc]
            go(p_copy(j, g))

    def place(long, s):
        if s == 0:
            return 0
        if long:
            return 7 if s == 4 else 2 * s - c
        return 2 * s - 1 + c

    def z_copy(j, long, s):
        index = (s - 1) if long else (3 + s)
        return remote(
            z_out.at[index, :, CUTS[j]], z_in.at[index, :, CUTS[j]], z_send.at[j, index], z_recv.at[j, index],
            z=z_short if long else z_long,
        )

    def both(j, at):
        g, i = (0, 0) if isinstance(at, int) and at == 0 else (at // 4, at % 4)
        return sums[g, c, i, :, CUTS[j]].astype(F32) + p_in[g, i, :, CUTS[j]].astype(F32)

    def z_stage(j, s):
        if s == 4:
            for g in range(2):
                p_copy(j, g).wait_recv()
        for long in ((True, False) if s < 4 else (True,)):
            index = (s - 1) if long else (3 + s)
            total = both(j, place(long, s))
            if s < (4 if long else 3):
                z_copy(j, long, s + 1).wait_recv()
                total = total + z_in[index + 1, :, CUTS[j]].astype(F32)
            z_out[index, :, CUTS[j]] = total.astype(BF)
            go(z_copy(j, long, s))

    def f_copy(j, m):
        return remote(
            f_out.at[:, CUTS[j]], f_in.at[m - 1, :, CUTS[j]], f_send.at[j, m - 1], f_recv.at[j, m - 1], x=(x + m) % NX
        )

    def home_stage(j):
        total = both(j, 0)
        for long in (True, False):
            z_copy(j, long, 1).wait_recv()
            total = total + z_in[0 if long else 4, :, CUTS[j]].astype(F32)
        f_out[:, CUTS[j]] = total.astype(BF)
        for m in (2, 1, 3):
            go(f_copy(j, m))

    def end_stage(j):
        for m in (1, 3, 2):
            f_copy(j, m).wait_recv()
        cut = CUTS[j]
        there = pl.ds(pl.multiple_of((1 - h) * HALF + cut.start, 128), cut.size)
        here = pl.ds(pl.multiple_of(h * HALF + cut.start, 128), cut.size)
        grads[:, there] = (f_in[0, :, cut].astype(F32) + f_in[2, :, cut].astype(F32)).astype(BF)
        grads[:, here] = (f_out[:, cut].astype(F32) + f_in[1, :, cut].astype(F32)).astype(BF)

    def g_copy(m):
        return remote(b_out, b_all.at[x], g_send.at[m], g_recv.at[x], x=(x + m) % NX)

    def gate_stage():
        for at in range(NZ):
            for far, cc in ((0, c), (1, other)):
                if at == 0 and far == 0:
                    continue
                remote(
                    v_out.at[at, cc], v_in.at[at, cc], v_send.at[at, far], v_recv.at[at, cc], c=other
                ).wait_recv()
        v_in[0, c] = v_out[0, c]
        row = lax.broadcasted_iota(jnp.int32, (16, TOK), 0)
        base = (y + row // LE) % NY * (NZ * NC * LE) + row % LE
        base = jnp.where(row < NY * LE, base, -NZ * NC * LE)
        found = [jnp.zeros((16, TOK), F32) for _ in range(8)]
        for r in range(NZ):
            for cc in range(NC):
                expert = (base + ((z + r) % NZ * NC + cc) * LE).astype(F32)
                value = v_in[PLACE[r], cc].astype(F32)
                for k in range(8):
                    same = info[k : k + 1].astype(F32) == expert
                    found[k] = jnp.where(same, value, found[k])
        for k in range(8):
            total = jnp.sum(found[k], axis=0, keepdims=True)
            b_out[k : k + 1] = total.astype(BF)
            b_out[8 + k : 9 + k] = total.astype(BF)
        for m in range(1, NX):
            go(g_copy(m))

    events = [(9.0, 0, turn, ()), (33.0, 0, gate_stage, ())]
    events += [(10.0 + 2 * n, 0, weight_stage, (n // 4, n % 4)) for n in range(8)]
    for j, cut in enumerate(CUTS):
        wide = cut.size / 256
        at = 8 + 32 * (cut.start + cut.size) / HALF
        events += [(at, j, x_stage, (j,)), (at + 1.5 + 2 * wide, j, relay_stage, (j,))]
        at += 3 + 7 * wide
        events.append((at, j, sum_stage, (j,)))
        at += 1 + 1.5 * wide
        for n in (4, 3, 2, 1):
            events.append((at, j, z_stage, (j, n)))
            at += 1.5 + 1.6 * wide
        events += [(at, j, home_stage, (j,)), (at + 2 + 3 * wide, j, end_stage, (j,))]
    for _, _, stage, given in sorted(events, key=lambda e: (e[0], e[1])):
        stage(*given)
    b_all[x] = b_out[...]
    for m in range(1, NX):
        at = (x + NX - m) % NX
        remote(b_out, b_all.at[at], g_send.at[m], g_recv.at[at], x=x_up).wait_recv()
    total = (
        b_all[0].astype(F32) + b_all[1].astype(F32) + b_all[2].astype(F32) + b_all[3].astype(F32)
    )
    grad_probs[...] = total[:8] / info[...].astype(F32)[8:]
    for i in range(3):
        for le in range(LE):
            for q in range(4):
                grad_copy(i, le, q).wait()
    for copy in waits:
        copy.wait_send()


def give_back(rows, pick, pick_t, inner, w_gate, w_up, probs, info):
    hid = w_gate.shape[1]
    count = NY * 2 * GROUP
    vmem = pl.BlockSpec(memory_space=pltpu.VMEM)
    anyw = pl.BlockSpec(memory_space=pl.ANY)
    dma = pltpu.SemaphoreType.DMA
    return pl.pallas_call(
        return_kernel,
        out_shape=(
            jax.ShapeDtypeStruct((TOK, 2 * HALF), BF),
            jax.ShapeDtypeStruct((8, TOK), F32),
            jax.ShapeDtypeStruct(w_gate.shape, BF),
            jax.ShapeDtypeStruct(w_gate.shape, BF),
            jax.ShapeDtypeStruct(w_gate.shape, BF),
        ),
        in_specs=[anyw, anyw, anyw, vmem, anyw, anyw, vmem, vmem],
        out_specs=(vmem, vmem, anyw, anyw, anyw),
        scratch_shapes=[
            pltpu.VMEM((8, LE, NY, 2, GROUP, LANES), BF),
            pltpu.VMEM((2, LE, 2, hid, HALF), BF),
            pltpu.VMEM((LE, 3, hid, count), BF),
            pltpu.VMEM((3, LE, 4, hid, LANES), BF),
            pltpu.VMEM((LE, NY, 2, GROUP, HALF), BF),
            pltpu.VMEM((LE, NY, 2, GROUP, HALF), BF),
            pltpu.VMEM((LE, NY, 2, GROUP, HALF), BF),
            pltpu.VMEM((2, NY, LE, GROUP, HALF), BF),
            pltpu.VMEM((LE, 2, GROUP, HALF), BF),
            pltpu.VMEM((2, NY * LE * GROUP, 4 * NC * TOK), BF),
            pltpu.VMEM((2, 4 * NC * TOK, NY * LE * GROUP), BF),
            pltpu.VMEM((2, NC, 4, TOK, HALF), BF),
            pltpu.VMEM((2, 4, TOK, HALF), BF),
            pltpu.VMEM((7, TOK, HALF), BF),
            pltpu.VMEM((7, TOK, HALF), BF),
            pltpu.VMEM((TOK, HALF), BF),
            pltpu.VMEM((3, TOK, HALF), BF),
            pltpu.VMEM((NZ, NC, 16, TOK), BF),
            pltpu.VMEM((NZ, NC, 16, TOK), BF),
            pltpu.VMEM((NY, LE, 2, 16, TOK), BF),
            pltpu.VMEM((NX, 16, TOK), BF),
            pltpu.VMEM((16, TOK), BF),
            dma((8,)), dma((2, LE, 2)), dma((3, LE, 4)),
            dma((4, LE)), dma((4, LE)),
            dma((4, 3, LE)), dma((4, 3, LE)),
            dma((4, LE)), dma((4, LE)),
            dma((4, 2)), dma((4, 2)),
            dma((4, 7)), dma((4, 7)),
            dma((4, 3)), dma((4, 3)),
            dma((NY,)), dma((NY,)),
            dma((NZ, 2)), dma((NZ, NC)),
            dma((NX,)), dma((NX,)), dma((2,)),
        ],
        compiler_params=pltpu.CompilerParams(
            collective_id=1, has_side_effects=True, vmem_limit_bytes=58 << 20
        ),
        name="give_back",
    )(rows, pick, pick_t, inner, w_gate, w_up, probs, info)


def body(tokens, grad_out, routes, probs, w_gate, w_up, w_down):
    info = jnp.concatenate([routes.T.astype(BF), probs.T], axis=0)
    rows, pick, pick_t, inner, prob = dispatch(
        tokens, grad_out, info, w_gate, w_up, w_down
    )
    grad_tokens, grad_probs, g_gate, g_up, g_down = give_back(
        rows, pick, pick_t, inner, w_gate, w_up, prob, info
    )
    return (grad_tokens, grad_probs.T.astype(BF), g_gate, g_up, g_down)


def solution(mesh):
    cut = Mesh(mesh.devices.reshape(NY, NZ, NC, NX), ("y", "z", "c", "x"))
    rows = P(("y", "z", "c"), None)
    weights = P(("y", "z", "c"), "x", None)
    return jax.shard_map(
        body,
        mesh=cut,
        in_specs=(rows, rows, rows, rows, weights, weights, weights),
        out_specs=(rows, rows, weights, weights, weights),
        check_vma=False,
    )
```
